512 devices in a mesh: grp: 8 (over x, y_lo), par: 64 (over z, y_hi, core).
Axes of the slice: x: 4, y: 4 (y_hi: 2, y_lo: 2; y = y_hi * 2 + y_lo), z: 16, core: 2. Of those that a mesh axis runs over, the one named last changes fastest.
Arguments:
- omega: bfloat16 [32, 524288], P(None, 'par'), may hold values from -6 to 6
- jac_blocks: bfloat16 [8, 8192, 128, 128], P('grp', 'par'), may hold values from -0.1796875 to 0.1796875
- block_param: int32 [8, 8192], P('grp', 'par'), may hold values from 0 to 63
- block_obs: int32 [8, 8192], P('grp', 'par'), may hold values from 0 to 63
- block_count: int32 [8, 64], P('grp', 'par'), may hold values from 16 to 128, as said below
- obs_weight: float32 [8, 8192], P('grp'), may hold values from 0.1 to 1
Outputs:
- hess_probe: float32 [32, 524288], P(None, ('par', 'grp'))
The draws below stay inside these ranges and needn't reach their ends.
Inputs may be any that keep to these rules, and one draw needn't show every extreme that they name: `block_count`: in every group four devices use all 128 slots and one device uses the fewest; the others use at most 64.
All inputs are finite; a program needn't handle non-finite values.
Results may differ from the reference program's by a relative error of at most 0.0027.
Values may be sent and summed in bfloat16 or wider, within the bound.
No kernel may reach another device: no remote copies, remote signals or barrier semaphores. Data moves between devices by JAX's collectives and lax.ppermute only.
A program may use at most 64 MiB of HBM per device.

```python
import math
import jax
import jax.numpy as jnp
from jax import lax

K = 32
BLK = 128
PB = 64
CAP = 128
OB = 64
GROUPS = 8
NPAR = 524288
OBS = 8192
SLOTS = 8192
N_GRP = 8
N_PAR = 64


def draw_block_count(key, part):
    first = jax.random.fold_in(key, 11)
    second = jax.random.fold_in(key, 23)
    lower = max(1, CAP // 8)
    base = jax.random.randint(first, (N_GRP, N_PAR), lower, CAP // 2 + 1)
    scores = jax.random.randint(second, (N_GRP, N_PAR), 0, 1 << 20) * N_PAR + jnp.arange(N_PAR, dtype=jnp.int32)[None, :]
    ranks = jnp.argsort(jnp.argsort(scores, axis=1), axis=1)
    counts = jnp.where(ranks < 4, CAP, base)
    counts = jnp.where(ranks == 4, lower, counts)
    return counts.astype(jnp.int32)


def plant(values, stream_key, low, largest):
    longest = values.shape.index(max(values.shape))
    spots = []
    for shift in (0, 1):
        where = [jax.random.randint(jax.random.fold_in(stream_key, axis), (), 0, length) for axis, length in enumerate(values.shape)]
        where[longest] = (where[longest] + shift) % values.shape[longest]
        spots.append(tuple(where))
    return values.at[spots[0]].set(low).at[spots[1]].set(largest)


def block_scale(rng, extent, shards, smallest, largest):
    gain, own = 1.0, jax.random.fold_in(rng, 6)
    for axis_at, blocks in shards:
        steps = jnp.exp(jax.random.uniform(jax.random.fold_in(own, axis_at), (blocks,), jnp.float32, smallest / len(shards), largest / len(shards)))
        gain = gain * jnp.repeat(steps, extent[axis_at] // blocks).reshape([-1 if axis == axis_at else 1 for axis in range(len(extent))])
    return gain


def bell_draw(key, extent, spread, bound, split=(), held_as=jnp.bfloat16):
    array = spread * jax.random.normal(key, extent, jnp.float32)
    if split:
        array = array * block_scale(key, extent, split, -0.22, 0.18)
    return jnp.clip(array, -bound, bound).astype(held_as)


def setup_inputs(seed: int = 0) -> dict:
    seeds = jax.random.split(jax.random.key(seed), 7)
    omega = bell_draw(seeds[0], (K, NPAR), 1.0, 6.0, ((1, 64),))
    jac_blocks = bell_draw(seeds[1], (GROUPS, SLOTS, BLK, BLK), 0.03, 0.1796875, ((0, 8), (1, 64)))
    block_param = plant(jax.random.randint(seeds[2], (GROUPS, SLOTS), 0, PB), jax.random.fold_in(seeds[2], 1), 0, PB - 1).astype(jnp.int32)
    block_obs = plant(jax.random.randint(seeds[3], (GROUPS, SLOTS), 0, OB), jax.random.fold_in(seeds[3], 1), 0, OB - 1).astype(jnp.int32)
    block_count = draw_block_count(jax.random.fold_in(seeds[6], 71), 0)
    obs_weight = jnp.clip(jnp.exp(math.log(1.0) - 2.3025851 * jax.random.uniform(seeds[5], (GROUPS, OBS), jnp.float32) ** block_scale(seeds[5], (GROUPS, OBS), ((0, 8),), -0.2, 0.2)), 0.1, 1.0)
    return dict(omega=omega, jac_blocks=jac_blocks, block_param=block_param, block_obs=block_obs, block_count=block_count, obs_weight=obs_weight)


def reference(omega, jac_blocks, block_param, block_obs, block_count, obs_weight):
    n_par = N_PAR
    slots = CAP * n_par
    panels = omega.reshape(K, n_par * PB, BLK)
    shard = jnp.arange(slots, dtype=jnp.int32) // CAP
    within = jnp.arange(slots, dtype=jnp.int32) % CAP

    def one_group(total, inputs):
        blocks, bparam, bobs, counts, weights = inputs
        active = (within < counts[shard]).astype(jnp.float32)
        gidx = (shard * PB + bparam).astype(jnp.int32)
        picked = jnp.take(panels, gidx, axis=1).astype(jnp.float32)
        terms = jnp.einsum("kcp,cpo->cko", picked, blocks.astype(jnp.float32))
        terms = terms * active[:, None, None]
        fwd = jax.ops.segment_sum(terms, bobs, num_segments=OB)
        fwd = jnp.transpose(fwd, (1, 0, 2)).reshape(K, OB * BLK)
        scaled = (fwd * weights[None, :]).astype(jnp.bfloat16)
        vblocks = scaled.reshape(K, OB, BLK)
        pickv = jnp.take(vblocks, bobs, axis=1).astype(jnp.float32)
        back = jnp.einsum("kco,cpo->ckp", pickv, blocks.astype(jnp.float32))
        back = back * active[:, None, None]
        summed = jax.ops.segment_sum(back, gidx, num_segments=n_par * PB)
        summed = jnp.transpose(summed, (1, 0, 2)).reshape(K, n_par * PB * BLK)
        return total + summed, None

    start = jnp.zeros((K, n_par * PB * BLK), jnp.float32)
    result, _ = lax.scan(one_group, start, (jac_blocks, block_param, block_obs, block_count, obs_weight))
    return result
```

```python
import jax
import jax.numpy as jnp
from jax import lax
from jax.experimental import pallas as pl
from jax.experimental.pallas import tpu as pltpu
from jax.sharding import Mesh, PartitionSpec as P

CHUNK = 16
PAR = ("z", "yh", "core")
GRP = ("x", "yl")


def fetch(n, jac_hbm, buf, sems):
    def copy(c):
        at = pl.ds(pl.multiple_of(c * CHUNK, CHUNK), CHUNK)
        return pltpu.make_async_copy(jac_hbm.at[0, at], buf.at[at], sems.at[c])

    for c in range(buf.shape[0] // CHUNK):

        @pl.when(c * CHUNK < n)
        def _():
            copy(c).start()

    return copy


def fwd_kernel(cnt_ref, bp_ref, bo_ref, omega_ref, jac_hbm, out_ref, buf, sems):
    width = buf.shape[1]
    n = cnt_ref[0, 0]
    copy = fetch(n, jac_hbm, buf, sems)
    out_ref[...] = jnp.zeros_like(out_ref)

    def step(c, carry):
        copy(c).wait()
        for j in range(CHUNK):
            s = c * CHUNK + j
            at = pl.multiple_of(bp_ref[0, s] * width, width)
            panel = omega_ref[:, pl.ds(at, width)]
            panel = jnp.where(s < n, panel, jnp.zeros_like(panel))
            term = jnp.dot(panel, buf[s], preferred_element_type=jnp.float32)
            o = bo_ref[0, s]
            out_ref[o] = out_ref[o] + term
        return carry

    lax.fori_loop(0, (n + CHUNK - 1) // CHUNK, step, 0)


def bwd_kernel(cnt_ref, bp_ref, bo_ref, v_ref, jac_hbm, out_ref, acc, buf, sems):
    n = cnt_ref[0, 0]
    copy = fetch(n, jac_hbm, buf, sems)
    acc[...] = jnp.zeros_like(acc)

    def step(c, carry):
        copy(c).wait()
        for j in range(CHUNK):
            s = c * CHUNK + j
            v = v_ref[bo_ref[0, s]]
            v = jnp.where(s < n, v, jnp.zeros_like(v))
            term = lax.dot_general(
                v, buf[s], (((1,), (1,)), ((), ())), preferred_element_type=jnp.float32
            )
            p = bp_ref[0, s]
            acc[p] = acc[p] + term
        return carry

    lax.fori_loop(0, (n + CHUNK - 1) // CHUNK, step, 0)
    out_ref[...] = acc[...].astype(out_ref.dtype)


def on_device(omega, jac_blocks, block_param, block_obs, block_count, obs_weight):
    probes = omega.shape[0]
    slots, width = jac_blocks.shape[1], jac_blocks.shape[2]
    pblocks = omega.shape[1] // width
    oblocks = obs_weight.shape[1] // width
    smem = pl.BlockSpec(memory_space=pltpu.SMEM)
    vmem = pl.BlockSpec(memory_space=pltpu.VMEM)
    hbm = pl.BlockSpec(memory_space=pltpu.HBM)
    blocks = pltpu.VMEM((slots, width, width), jac_blocks.dtype)
    done = pltpu.SemaphoreType.DMA((slots // CHUNK,))
    params = pltpu.CompilerParams(vmem_limit_bytes=24 << 20)

    partial_sum = pl.pallas_call(
        fwd_kernel,
        out_shape=jax.ShapeDtypeStruct((oblocks, probes, width), jnp.float32),
        in_specs=[smem, smem, smem, vmem, hbm],
        out_specs=vmem,
        scratch_shapes=[blocks, done],
        compiler_params=params,
        name="fwd_blocks",
    )(block_count, block_param, block_obs, omega, jac_blocks)

    def swap_sum(v, axes):
        n = lax.axis_size(axes)
        v = lax.all_to_all(v, axes, 0, 0, tiled=True)
        return jnp.sum(v.reshape(n, v.shape[0] // n, probes, width), axis=0)

    owned = swap_sum(partial_sum, "core")
    owned = swap_sum(owned, "yh")
    owned = swap_sum(owned, "z")
    mine = (lax.axis_index("core") * 2 + lax.axis_index("yh")) * 16 + lax.axis_index("z")
    weight = lax.dynamic_slice(obs_weight.reshape(oblocks, 1, width), (mine, 0, 0), (1, 1, width))
    scaled = (owned * weight).astype(jnp.bfloat16)
    nz = lax.axis_size("z")
    scaled = lax.all_to_all(jnp.broadcast_to(scaled, (nz, probes, width)), "z", 0, 0, tiled=True)
    scaled = lax.all_gather(scaled, "yh", axis=0, tiled=True)
    scaled = lax.all_gather(scaled, "core", axis=0, tiled=True)

    local_terms = pl.pallas_call(
        bwd_kernel,
        out_shape=jax.ShapeDtypeStruct((pblocks, probes, width), jnp.bfloat16),
        in_specs=[smem, smem, smem, vmem, hbm],
        out_specs=vmem,
        scratch_shapes=[pltpu.VMEM((pblocks, probes, width), jnp.float32), blocks, done],
        compiler_params=params,
        name="bwd_blocks",
    )(block_count, block_param, block_obs, scaled, jac_blocks)

    n = lax.axis_size(GRP)
    got = lax.all_to_all(local_terms, GRP, 0, 0, tiled=True)
    got = got.reshape(n, pblocks // n, probes, width).astype(jnp.float32)
    total = jnp.sum(got, axis=0)
    return jnp.transpose(total, (1, 0, 2)).reshape(probes, pblocks // n * width)


def solution(mesh):
    mesh = Mesh(mesh.devices.reshape(4, 2, 16, 2, 2), GRP + PAR)
    in_specs = (
        P(None, PAR),
        P(GRP, PAR, None, None),
        P(GRP, PAR),
        P(GRP, PAR),
        P(GRP, PAR),
        P(GRP, None),
    )
    out_specs = P(None, PAR + GRP)
    return jax.shard_map(
        on_device, mesh=mesh, in_specs=in_specs, out_specs=out_specs, check_vma=False
    )
```

```python
import jax
import jax.numpy as jnp
from jax import lax
from jax.experimental import pallas as pl
from jax.experimental.pallas import tpu as pltpu
from jax.sharding import Mesh, PartitionSpec as P

CHUNK = 16
SUB = 8
PAR = ("z", "yh", "core")
GRP = ("x", "yl")


def fetch(n, jac_hbm, jac, sems):
    def chunk(c):
        at = pl.ds(pl.multiple_of(c * CHUNK, CHUNK), CHUNK)
        return pltpu.make_async_copy(jac_hbm.at[0, at], jac.at[at], sems.at[c])

    for c in range(jac.shape[0] // CHUNK):

        @pl.when(c * CHUNK < n)
        def _():
            chunk(c).start()

    return chunk


def fwd_kernel(cnt, bp_hbm, bo_hbm, omega_hbm, jac_hbm, out_ref, bp, bo, jac, omega, sems, jsems):
    width = jac.shape[1]
    probes = omega.shape[0]
    half = (out_ref.shape[1] - SUB) // probes
    small = [
        pltpu.make_async_copy(src, dst, sems.at[i])
        for i, (src, dst) in enumerate(((bp_hbm, bp), (bo_hbm, bo), (omega_hbm, omega)))
    ]
    for copy in small:
        copy.start()

    n = cnt[0, 0]
    chunk = fetch(n, jac_hbm, jac, jsems)
    out_ref[...] = jnp.zeros_like(out_ref)
    for copy in small:
        copy.wait()

    def step(c, carry):
        chunk(c).wait()
        for j in range(CHUNK):
            s = c * CHUNK + j
            at = pl.multiple_of(bp[0, s] * width, width)
            panel = omega[:, pl.ds(at, width)]
            panel = jnp.where(s < n, panel, jnp.zeros_like(panel))
            term = jnp.dot(panel, jac[s], preferred_element_type=jnp.float32)
            o = bo[0, s]
            rows = pl.ds(pl.multiple_of((o % half) * probes, probes), probes)
            out_ref[o // half, rows] = out_ref[o // half, rows] + term
        return carry

    lax.fori_loop(0, (n + CHUNK - 1) // CHUNK, step, 0)
    body = out_ref.shape[1] - SUB
    top = jnp.zeros((SUB, width), jnp.float32)
    for i in range(2):
        top = jnp.maximum(top, jnp.max(jnp.abs(out_ref[i, :body].reshape(body // SUB, SUB, width)), axis=0))
    for i in range(2):
        out_ref[i, body:] = top


def pack_kernel(pair_ref, out_ref):
    rows = pair_ref.shape[1] - SUB
    parts, each, width = out_ref.shape
    each = each - SUB
    top = pair_ref[0, rows:] + pair_ref[1, rows:]
    power = jnp.clip(jnp.ceil(jnp.log2(top)), -100.0, 100.0) - 14.0
    data = pair_ref[0, :rows] + pair_ref[1, :rows]
    data = data.reshape(rows // SUB, SUB, width) * jnp.exp2(-power)
    out_ref[:, :each] = data.reshape(parts, each, width)
    out_ref[:, each:] = jnp.broadcast_to(power, (parts, SUB, width))


def bwd_kernel(cnt_ref, bp_ref, bo_ref, v_ref, jac_hbm, out_ref, acc, jac_ref, jsems):
    n = cnt_ref[0, 0]
    chunk = fetch(n, jac_hbm, jac_ref, jsems)
    acc[...] = jnp.zeros_like(acc)

    def step(c, carry):
        chunk(c).wait()
        for j in range(CHUNK):
            s = c * CHUNK + j
            v = v_ref[bo_ref[0, s]]
            v = jnp.where(s < n, v, jnp.zeros_like(v))
            term = lax.dot_general(
                v, jac_ref[s], (((1,), (1,)), ((), ())), preferred_element_type=jnp.float32
            )
            p = bp_ref[0, s]
            acc[p] = acc[p] + term
        return carry

    lax.fori_loop(0, (n + CHUNK - 1) // CHUNK, step, 0)
    out_ref[...] = acc[...].astype(out_ref.dtype)


def on_device(omega, jac_blocks, block_param, block_obs, block_count, obs_weight):
    probes = omega.shape[0]
    slots, width = jac_blocks.shape[1], jac_blocks.shape[2]
    pblocks = omega.shape[1] // width
    oblocks = obs_weight.shape[1] // width
    nz, nyh, ncore = (lax.axis_size(a) for a in PAR)
    smem = pl.BlockSpec(memory_space=pltpu.SMEM)
    vmem = pl.BlockSpec(memory_space=pltpu.VMEM)
    hbm = pl.BlockSpec(memory_space=pltpu.HBM)
    params = pltpu.CompilerParams(vmem_limit_bytes=24 << 20)
    blocks = pltpu.VMEM((slots, width, width), jac_blocks.dtype)
    done = pltpu.SemaphoreType.DMA((slots // CHUNK,))
    held = [
        pltpu.with_memory_space_constraint(a, pltpu.HBM)
        for a in (block_param, block_obs, omega, jac_blocks)
    ]
    rows = oblocks // ncore * probes
    partial_sum, bp, bo = pl.pallas_call(
        fwd_kernel,
        out_shape=(
            jax.ShapeDtypeStruct((ncore, rows + SUB, width), jnp.float32),
            jax.ShapeDtypeStruct(block_param.shape, jnp.int32),
            jax.ShapeDtypeStruct(block_obs.shape, jnp.int32),
        ),
        in_specs=[smem] + [hbm] * 4,
        out_specs=(vmem, smem, smem),
        scratch_shapes=[
            blocks,
            pltpu.VMEM(omega.shape, omega.dtype),
            pltpu.SemaphoreType.DMA((3,)),
            done,
        ],
        compiler_params=params,
        name="fwd_blocks",
    )(block_count, *held)

    each = rows // nz
    per = each // probes
    first = (lax.axis_index("core") * nz + lax.axis_index("z")) * per
    weight = lax.dynamic_slice(obs_weight.reshape(oblocks, 1, width), (first, 0, 0), (per, 1, width))
    partial_sum, weight = lax.optimization_barrier((partial_sum, weight))
    pair = lax.all_to_all(partial_sum, "core", 0, 0, tiled=True)
    packed = pl.pallas_call(
        pack_kernel,
        out_shape=jax.ShapeDtypeStruct((nz, each + SUB, width), jnp.float32),
        in_specs=[vmem],
        out_specs=vmem,
        compiler_params=pltpu.CompilerParams(vmem_limit_bytes=8 << 20),
        name="pair_sum_scaled",
    )(pair)
    got = lax.all_to_all(packed.astype(jnp.float16), "z", 0, 0, tiled=True)
    scale = jnp.exp2(got[:, each:].astype(jnp.float32))
    data = got[:, :each].astype(jnp.float32).reshape(nz, each // SUB, SUB, width)
    owned = jnp.sum(data * scale[:, None], axis=0).reshape(each // probes, probes, width)
    owned = owned + lax.ppermute(owned, "yh", [(i, nyh - 1 - i) for i in range(nyh)])

    scaled = (owned * weight).astype(jnp.bfloat16)
    scaled = jnp.broadcast_to(scaled, (nz, per, probes, width)).reshape(nz * per, probes, width)
    scaled = lax.all_to_all(scaled, "z", 0, 0, tiled=True)
    scaled = lax.all_gather(scaled, "core", axis=0, tiled=True)

    local_terms = pl.pallas_call(
        bwd_kernel,
        out_shape=jax.ShapeDtypeStruct((pblocks, probes, width), jnp.bfloat16),
        in_specs=[smem, smem, smem, vmem, hbm],
        out_specs=vmem,
        scratch_shapes=[pltpu.VMEM((pblocks, probes, width), jnp.float32), blocks, done],
        compiler_params=params,
        name="bwd_blocks",
    )(block_count, bp, bo, scaled, held[3])

    n = lax.axis_size(GRP)
    got = lax.all_to_all(local_terms, GRP, 0, 0, tiled=True)
    got = got.reshape(n, pblocks // n, probes, width).astype(jnp.float32)
    total = jnp.sum(got, axis=0)
    return jnp.transpose(total, (1, 0, 2)).reshape(probes, pblocks // n * width)


def solution(mesh):
    mesh = Mesh(mesh.devices.reshape(4, 2, 16, 2, 2), GRP + PAR)
    in_specs = (
        P(None, PAR),
        P(GRP, PAR, None, None),
        P(GRP, PAR),
        P(GRP, PAR),
        P(GRP, PAR),
        P(GRP, None),
    )
    out_specs = P(None, PAR + GRP)
    return jax.shard_map(
        on_device, mesh=mesh, in_specs=in_specs, out_specs=out_specs, check_vma=False
    )
```

```python
import jax
import jax.numpy as jnp
from jax import lax
from jax.experimental import pallas as pl
from jax.experimental.pallas import tpu as pltpu
from jax.sharding import Mesh, PartitionSpec as P

CHUNK = 16
SUB = 8
PAR = ("z", "yh", "core")
GRP = ("x", "yl")


def fetch(n, jac_hbm, jac, sems):
    def chunk(c):
        at = pl.ds(pl.multiple_of(c * CHUNK, CHUNK), CHUNK)
        return pltpu.make_async_copy(jac_hbm.at[0, at], jac.at[at], sems.at[c])

    for c in range(jac.shape[0] // CHUNK):

        @pl.when(c * CHUNK < n)
        def _():
            chunk(c).start()

    return chunk


def fwd_kernel(me, cnt, bp_hbm, bo_hbm, omega_hbm, jac_hbm, sums_ref, bp, bo, jac, omega, sems, jsems):
    width = jac.shape[1]
    probes = omega.shape[0]
    rows = sums_ref.shape[1] - SUB
    small = [
        pltpu.make_async_copy(src, dst, sems.at[i])
        for i, (src, dst) in enumerate(((bp_hbm, bp), (bo_hbm, bo), (omega_hbm, omega)))
    ]
    for copy in small:
        copy.start()
    n = cnt[0, 0]
    chunk = fetch(n, jac_hbm, jac, jsems)
    sums_ref[...] = jnp.zeros_like(sums_ref)
    flip = me[0, 0] * (rows // probes // 2)
    for copy in small:
        copy.wait()

    def step(c, carry):
        chunk(c).wait()
        for j in range(CHUNK):
            s = c * CHUNK + j
            at = pl.multiple_of(bp[0, s] * width, width)
            panel = omega[:, pl.ds(at, width)]
            panel = jnp.where(s < n, panel, jnp.zeros_like(panel))
            term = jnp.dot(panel, jac[s], preferred_element_type=jnp.float32)
            o = bo[0, s] ^ flip
            part = o // (rows // probes)
            at = pl.ds(pl.multiple_of(o % (rows // probes) * probes, probes), probes)
            sums_ref[part, at] = sums_ref[part, at] + term
        return carry

    lax.fori_loop(0, (n + CHUNK - 1) // CHUNK, step, 0)
    top = jnp.zeros((SUB, width), jnp.float32)
    for i in range(2):
        top = jnp.maximum(top, jnp.max(jnp.abs(sums_ref[i, :rows].reshape(rows // SUB, SUB, width)), axis=0))
    for i in range(2):
        sums_ref[i, rows:] = top


def core_kernel(sums_ref, got_ref, mine_ref, other_ref):
    half = mine_ref.shape[0]
    width = mine_ref.shape[1]
    top = sums_ref[0, 2 * half :] + got_ref[2 * half :]
    power = jnp.clip(jnp.ceil(jnp.log2(top)), -100.0, 100.0) - 14.0
    mine_ref[...] = sums_ref[0, :half] + got_ref[:half]
    other = sums_ref[0, half : 2 * half] + got_ref[half : 2 * half]
    other = other.reshape(half // SUB, SUB, width) * jnp.exp2(-power)
    other_ref[:half] = other.reshape(half, width)
    other_ref[half:] = power


def chip_kernel(mine_ref, sent_ref, got_ref, out_ref):
    parts, each, width = out_ref.shape
    each = each - SUB
    half = mine_ref.shape[0]
    theirs = got_ref[half:]
    power = jnp.maximum(sent_ref[half:], theirs) + 1.0
    got = got_ref[:half].reshape(half // SUB, SUB, width) * jnp.exp2(theirs - power)
    data = mine_ref[...].reshape(half // SUB, SUB, width) * jnp.exp2(-power) + got
    out_ref[:, :each] = data.reshape(parts, each, width)
    out_ref[:, each:] = jnp.broadcast_to(power, (parts, SUB, width))


def bwd_kernel(cnt_ref, bp_ref, bo_ref, v_ref, jac_hbm, out_ref, acc, jac_ref, jsems):
    n = cnt_ref[0, 0]
    chunk = fetch(n, jac_hbm, jac_ref, jsems)
    acc[...] = jnp.zeros_like(acc)

    def step(c, carry):
        chunk(c).wait()
        for j in range(CHUNK):
            s = c * CHUNK + j
            v = v_ref[bo_ref[0, s]]
            v = jnp.where(s < n, v, jnp.zeros_like(v))
            term = lax.dot_general(
                v, jac_ref[s], (((1,), (1,)), ((), ())), preferred_element_type=jnp.float32
            )
            p = bp_ref[0, s]
            acc[p] = acc[p] + term
        return carry

    lax.fori_loop(0, (n + CHUNK - 1) // CHUNK, step, 0)
    out_ref[...] = acc[...].astype(out_ref.dtype)


def on_device(omega, jac_blocks, block_param, block_obs, block_count, obs_weight):
    probes = omega.shape[0]
    slots, width = jac_blocks.shape[1], jac_blocks.shape[2]
    pblocks = omega.shape[1] // width
    oblocks = obs_weight.shape[1] // width
    nz, nyh, ncore = (lax.axis_size(a) for a in PAR)
    smem = pl.BlockSpec(memory_space=pltpu.SMEM)
    vmem = pl.BlockSpec(memory_space=pltpu.VMEM)
    hbm = pl.BlockSpec(memory_space=pltpu.HBM)
    little = pltpu.CompilerParams(vmem_limit_bytes=8 << 20)
    params = pltpu.CompilerParams(vmem_limit_bytes=24 << 20)
    blocks = pltpu.VMEM((slots, width, width), jac_blocks.dtype)
    done = pltpu.SemaphoreType.DMA((slots // CHUNK,))
    held = [
        pltpu.with_memory_space_constraint(a, pltpu.HBM)
        for a in (block_param, block_obs, omega, jac_blocks)
    ]
    rows = oblocks // ncore * probes
    each = oblocks // (nz * nyh * ncore) * probes
    per = each // probes
    quarter = lax.axis_index("core") * nyh + lax.axis_index("yh")
    weight = lax.dynamic_slice(
        obs_weight.reshape(oblocks, 1, width),
        ((quarter * nz + lax.axis_index("z")) * per, 0, 0),
        (per, 1, width),
    )
    sums, bp, bo = pl.pallas_call(
        fwd_kernel,
        out_shape=(
            jax.ShapeDtypeStruct((ncore, rows + SUB, width), jnp.float32),
            jax.ShapeDtypeStruct(block_param.shape, jnp.int32),
            jax.ShapeDtypeStruct(block_obs.shape, jnp.int32),
        ),
        in_specs=[smem] * 2 + [hbm] * 4,
        out_specs=(vmem, smem, smem),
        scratch_shapes=[
            blocks,
            pltpu.VMEM(omega.shape, omega.dtype),
            pltpu.SemaphoreType.DMA((3,)),
            done,
        ],
        compiler_params=params,
        name="fwd_blocks",
    )(quarter.reshape(1, 1), block_count, *held)
    sums, weight = lax.optimization_barrier((sums, weight))

    swap = [(i, 1 - i) for i in range(2)]
    mine, other = pl.pallas_call(
        core_kernel,
        out_shape=(
            jax.ShapeDtypeStruct((rows // nyh, width), jnp.float32),
            jax.ShapeDtypeStruct((rows // nyh + SUB, width), jnp.float32),
        ),
        in_specs=[vmem] * 2,
        out_specs=(vmem, vmem),
        compiler_params=little,
        name="add_core",
    )(sums, lax.ppermute(sums[1], "core", swap))
    got = lax.ppermute(other.astype(jnp.float16), "yh", swap).astype(jnp.float32)
    packed = pl.pallas_call(
        chip_kernel,
        out_shape=jax.ShapeDtypeStruct((nz, each + SUB, width), jnp.float32),
        in_specs=[vmem] * 3,
        out_specs=vmem,
        compiler_params=little,
        name="add_chip",
    )(mine, other, got)
    got = lax.all_to_all(packed.astype(jnp.float16), "z", 0, 0, tiled=True)
    scale = jnp.exp2(got[:, each:].astype(jnp.float32))
    data = got[:, :each].astype(jnp.float32).reshape(nz, each // SUB, SUB, width)
    owned = jnp.sum(data * scale[:, None], axis=0).reshape(per, probes, width)

    scaled = (owned * weight).astype(jnp.bfloat16)
    scaled = jnp.broadcast_to(scaled, (nz, per, probes, width)).reshape(nz * per, probes, width)
    scaled = lax.all_to_all(scaled, "z", 0, 0, tiled=True)
    scaled = lax.all_gather(scaled, "yh", axis=0, tiled=True)
    scaled = lax.all_gather(scaled, "core", axis=0, tiled=True)

    local_terms = pl.pallas_call(
        bwd_kernel,
        out_shape=jax.ShapeDtypeStruct((pblocks, probes, width), jnp.bfloat16),
        in_specs=[smem, smem, smem, vmem, hbm],
        out_specs=vmem,
        scratch_shapes=[pltpu.VMEM((pblocks, probes, width), jnp.float32), blocks, done],
        compiler_params=params,
        name="bwd_blocks",
    )(block_count, bp, bo, scaled, held[3])

    n = lax.axis_size(GRP)
    got = lax.all_to_all(local_terms, GRP, 0, 0, tiled=True)
    got = got.reshape(n, pblocks // n, probes, width).astype(jnp.float32)
    total = jnp.sum(got, axis=0)
    return jnp.transpose(total, (1, 0, 2)).reshape(probes, pblocks // n * width)


def solution(mesh):
    mesh = Mesh(mesh.devices.reshape(4, 2, 16, 2, 2), GRP + PAR)
    in_specs = (
        P(None, PAR),
        P(GRP, PAR, None, None),
        P(GRP, PAR),
        P(GRP, PAR),
        P(GRP, PAR),
        P(GRP, None),
    )
    out_specs = P(None, PAR + GRP)
    return jax.shard_map(
        on_device, mesh=mesh, in_specs=in_specs, out_specs=out_specs, check_vma=False
    )
```

```python
import jax
import jax.numpy as jnp
from jax import lax
from jax.experimental import pallas as pl
from jax.experimental.pallas import tpu as pltpu
from jax.sharding import Mesh, PartitionSpec as P

CHUNK = 64
FETCH = 16
SUB = 8
PAR = ("z", "yh", "core")
GRP = ("x", "yl")


def fwd_kernel(
    me, cnt, bp_hbm, bo_hbm, omega_hbm, jac_hbm, sums_ref, jac, bp, bo, omega, sems, jsems
):
    width = jac.shape[1]
    probes = omega.shape[0]
    rows = sums_ref.shape[1] - SUB
    half = rows // probes
    small = [
        pltpu.make_async_copy(src, dst, sems.at[i])
        for i, (src, dst) in enumerate(((bp_hbm, bp), (bo_hbm, bo), (omega_hbm, omega)))
    ]
    for copy in small:
        copy.start()
    n = cnt[0, 0]

    def piece(c):
        at = pl.ds(c * FETCH, FETCH)
        return pltpu.make_async_copy(jac_hbm.at[0, at], jac.at[at], jsems.at[c])

    def each_piece(act):
        for first in range(0, jac.shape[0], CHUNK):
            pieces = range(first // FETCH, (first + CHUNK) // FETCH)
            if first:

                @pl.when(first < n)
                def _():
                    for c in pieces:
                        act(c, first + CHUNK)
            else:
                for c in pieces:
                    act(c, first + CHUNK)

    each_piece(lambda c, end: piece(c).start())
    sums_ref[...] = jnp.zeros_like(sums_ref)
    for copy in small:
        copy.wait()

    def use(c, end):
        piece(c).wait()
        for s in range(c * FETCH, (c + 1) * FETCH):
            at = pl.multiple_of(bp[0, s] * width, width)
            panel = omega[:, pl.ds(at, width)]
            panel = jnp.where(s < n, panel, jnp.zeros_like(panel))
            term = jnp.dot(panel, jac[s], preferred_element_type=jnp.float32)
            o = bo[0, s]
            part = (o // half) ^ me[0, 0]
            row = (o % (half // 2)) * 2 + o // (half // 2) % 2
            at = pl.ds(pl.multiple_of(row * probes, probes), probes)
            sums_ref[part, at] = sums_ref[part, at] + term

    each_piece(use)
    top = jnp.zeros((SUB, width), jnp.float32)
    for i in range(2):
        top = jnp.maximum(top, jnp.max(jnp.abs(sums_ref[i, :rows].reshape(rows // SUB, SUB, width)), axis=0))
    for i in range(2):
        sums_ref[i, rows:] = top


def core_kernel(sums_ref, got_ref, out_ref):
    parts, each, width = out_ref.shape
    each = each - SUB
    rows = parts * each
    top = sums_ref[0, rows:] + got_ref[rows:]
    power = jnp.clip(jnp.ceil(jnp.log2(top)), -100.0, 100.0) - 14.0
    data = (sums_ref[0, :rows] + got_ref[:rows]).reshape(rows // SUB, SUB, width) * jnp.exp2(-power)
    out_ref[:, :each] = data.reshape(parts, each, width)
    out_ref[:, each:] = jnp.broadcast_to(power, (parts, SUB, width))


def bwd_kernel(cnt, bp, bo, v_ref, jac, out_ref, acc):
    width = jac.shape[1]
    probes = v_ref.shape[1]
    n = cnt[0, 0]
    acc[...] = jnp.zeros_like(acc)

    def step(c, carry):
        for j in range(0, CHUNK, 2):
            first = c * CHUNK + j
            pair = []
            for s in (first, first + 1):
                v = v_ref[bo[0, s]]
                pair.append(jnp.where(s < n, v, jnp.zeros_like(v)))
            blocks = jac[pl.ds(first, 2)].reshape(2 * width, width)
            terms = lax.dot_general(
                jnp.concatenate(pair, axis=0),
                blocks,
                (((1,), (1,)), ((), ())),
                preferred_element_type=jnp.float32,
            )
            for i in range(2):
                p = bp[0, first + i]
                acc[p] = acc[p] + terms[i * probes : (i + 1) * probes, i * width : (i + 1) * width]
        return carry

    lax.fori_loop(0, (n + CHUNK - 1) // CHUNK, step, 0)
    out_ref[...] = acc[...].astype(out_ref.dtype)


def on_device(omega, jac_blocks, block_param, block_obs, block_count, obs_weight):
    probes = omega.shape[0]
    slots, width = jac_blocks.shape[1], jac_blocks.shape[2]
    pblocks = omega.shape[1] // width
    oblocks = obs_weight.shape[1] // width
    nz, nyh, ncore = (lax.axis_size(a) for a in PAR)
    smem = pl.BlockSpec(memory_space=pltpu.SMEM)
    vmem = pl.BlockSpec(memory_space=pltpu.VMEM)
    hbm = pl.BlockSpec(memory_space=pltpu.HBM)
    little = pltpu.CompilerParams(vmem_limit_bytes=8 << 20)
    params = pltpu.CompilerParams(vmem_limit_bytes=24 << 20)
    held = [
        pltpu.with_memory_space_constraint(a, pltpu.HBM)
        for a in (block_param, block_obs, omega, jac_blocks)
    ]
    rows = oblocks // ncore * probes
    each = oblocks // (nz * nyh * ncore) * probes
    per = each // probes
    quarter = lax.axis_index("core") * nyh + lax.axis_index("yh")
    weight = lax.dynamic_slice(
        obs_weight.reshape(oblocks, 1, width),
        ((quarter * nz + lax.axis_index("z")) * per, 0, 0),
        (per, 1, width),
    )
    sums, jac, bp, bo = pl.pallas_call(
        fwd_kernel,
        out_shape=(
            jax.ShapeDtypeStruct((ncore, rows + SUB, width), jnp.float32),
            jax.ShapeDtypeStruct((slots, width, width), jac_blocks.dtype),
            jax.ShapeDtypeStruct(block_param.shape, jnp.int32),
            jax.ShapeDtypeStruct(block_obs.shape, jnp.int32),
        ),
        in_specs=[smem] * 2 + [hbm] * 4,
        out_specs=(vmem, vmem, smem, smem),
        scratch_shapes=[
            pltpu.VMEM(omega.shape, omega.dtype),
            pltpu.SemaphoreType.DMA((3,)),
            pltpu.SemaphoreType.DMA((slots // FETCH,)),
        ],
        compiler_params=params,
        name="fwd_blocks",
    )(lax.axis_index("core").reshape(1, 1), block_count, *held)
    sums, weight = lax.optimization_barrier((sums, weight))

    packed = pl.pallas_call(
        core_kernel,
        out_shape=jax.ShapeDtypeStruct((nz * nyh, each + SUB, width), jnp.float32),
        in_specs=[vmem] * 2,
        out_specs=vmem,
        compiler_params=little,
        name="add_core",
    )(sums, lax.ppermute(sums[1], "core", [(0, 1), (1, 0)]))
    got = lax.all_to_all(packed.astype(jnp.float16), ("z", "yh"), 0, 0, tiled=True)
    scale = jnp.exp2(got[:, each:].astype(jnp.float32))
    data = got[:, :each].astype(jnp.float32).reshape(nz * nyh, each // SUB, SUB, width)
    owned = jnp.sum(data * scale[:, None], axis=0).reshape(per, probes, width)

    scaled = (owned * weight).astype(jnp.bfloat16)
    scaled = jnp.broadcast_to(scaled, (nz, per, probes, width)).reshape(nz * per, probes, width)
    scaled = lax.all_to_all(scaled, "z", 0, 0, tiled=True)
    scaled = lax.all_gather(scaled, "yh", axis=0, tiled=True)
    scaled = lax.all_gather(scaled, "core", axis=0, tiled=True)

    local_terms = pl.pallas_call(
        bwd_kernel,
        out_shape=jax.ShapeDtypeStruct((pblocks, probes, width), jnp.bfloat16),
        in_specs=[smem, smem, smem, vmem, vmem],
        out_specs=vmem,
        scratch_shapes=[pltpu.VMEM((pblocks, probes, width), jnp.float32)],
        compiler_params=params,
        name="bwd_blocks",
    )(block_count, bp, bo, scaled, jac)

    n = lax.axis_size(GRP)
    got = lax.all_to_all(local_terms, GRP, 0, 0, tiled=True)
    got = got.reshape(n, pblocks // n, probes, width).astype(jnp.float32)
    total = jnp.sum(got, axis=0)
    return jnp.transpose(total, (1, 0, 2)).reshape(probes, pblocks // n * width)


def solution(mesh):
    mesh = Mesh(mesh.devices.reshape(4, 2, 16, 2, 2), GRP + PAR)
    in_specs = (
        P(None, PAR),
        P(GRP, PAR, None, None),
        P(GRP, PAR),
        P(GRP, PAR),
        P(GRP, PAR),
        P(GRP, None),
    )
    out_specs = P(None, PAR + GRP)
    return jax.shard_map(
        on_device, mesh=mesh, in_specs=in_specs, out_specs=out_specs, check_vma=False
    )
```

```python
import jax
import jax.numpy as jnp
from jax import lax
from jax.experimental import pallas as pl
from jax.experimental.pallas import tpu as pltpu
from jax.sharding import Mesh, PartitionSpec as P

CHUNK = 64
SUB = 8
PAR = ("z", "yh", "core")
GRP = ("x", "yl")


def fwd_kernel(
    me, cnt, bp_hbm, bo_hbm, omega_hbm, jac_hbm, sums_ref, jac, bp, bo, omega, sems, jsems
):
    width = jac.shape[1]
    probes = omega.shape[0]
    rows = sums_ref.shape[1] - SUB
    half = rows // probes
    small = [
        pltpu.make_async_copy(src, dst, sems.at[i])
        for i, (src, dst) in enumerate(((bp_hbm, bp), (bo_hbm, bo), (omega_hbm, omega)))
    ]
    for copy in small:
        copy.start()
    n = cnt[0, 0]

    def chunk(c):
        at = pl.ds(pl.multiple_of(c * CHUNK, CHUNK), CHUNK)
        return pltpu.make_async_copy(jac_hbm.at[0, at], jac.at[at], jsems.at[c])

    for c in range(jac.shape[0] // CHUNK):

        @pl.when(c * CHUNK < n)
        def _():
            chunk(c).start()

    sums_ref[...] = jnp.zeros_like(sums_ref)
    flip = me[0, 0] * (half // 2)
    for copy in small:
        copy.wait()

    def step(c, carry):
        chunk(c).wait()
        for j in range(CHUNK):
            s = c * CHUNK + j
            at = pl.multiple_of(bp[0, s] * width, width)
            panel = omega[:, pl.ds(at, width)]
            panel = jnp.where(s < n, panel, jnp.zeros_like(panel))
            term = jnp.dot(panel, jac[s], preferred_element_type=jnp.float32)
            o = bo[0, s] ^ flip
            at = pl.ds(pl.multiple_of(o % half * probes, probes), probes)
            sums_ref[o // half, at] = sums_ref[o // half, at] + term
        return carry

    lax.fori_loop(0, (n + CHUNK - 1) // CHUNK, step, 0)
    top = jnp.zeros((SUB, width), jnp.float32)
    for i in range(2):
        top = jnp.maximum(top, jnp.max(jnp.abs(sums_ref[i, :rows].reshape(rows // SUB, SUB, width)), axis=0))
    for i in range(2):
        sums_ref[i, rows:] = top


def core_kernel(sums_ref, got_ref, mine_ref, other_ref):
    half = mine_ref.shape[0]
    width = mine_ref.shape[1]
    top = sums_ref[0, 2 * half :] + got_ref[2 * half :]
    power = jnp.clip(jnp.ceil(jnp.log2(top)), -100.0, 100.0) - 14.0
    mine_ref[...] = sums_ref[0, :half] + got_ref[:half]
    other = sums_ref[0, half : 2 * half] + got_ref[half : 2 * half]
    other = other.reshape(half // SUB, SUB, width) * jnp.exp2(-power)
    other_ref[:half] = other.reshape(half, width)
    other_ref[half:] = power


def chip_kernel(mine_ref, sent_ref, got_ref, out_ref):
    parts, each, width = out_ref.shape
    each = each - SUB
    half = mine_ref.shape[0]
    theirs = got_ref[half:]
    power = jnp.maximum(sent_ref[half:], theirs) + 1.0
    got = got_ref[:half].reshape(half // SUB, SUB, width) * jnp.exp2(theirs - power)
    data = mine_ref[...].reshape(half // SUB, SUB, width) * jnp.exp2(-power) + got
    out_ref[:, :each] = data.reshape(parts, each, width)
    out_ref[:, each:] = jnp.broadcast_to(power, (parts, SUB, width))


def bwd_kernel(cnt, bp, bo, v_ref, jac, out_ref, acc):
    width = jac.shape[1]
    probes = v_ref.shape[1]
    n = cnt[0, 0]
    acc[...] = jnp.zeros_like(acc)

    def step(c, carry):
        for j in range(0, CHUNK, 2):
            first = c * CHUNK + j
            pair = []
            for s in (first, first + 1):
                v = v_ref[bo[0, s]]
                pair.append(jnp.where(s < n, v, jnp.zeros_like(v)))
            blocks = jac[pl.ds(first, 2)].reshape(2 * width, width)
            terms = lax.dot_general(
                jnp.concatenate(pair, axis=0),
                blocks,
                (((1,), (1,)), ((), ())),
                preferred_element_type=jnp.float32,
            )
            for i in range(2):
                p = bp[0, first + i]
                acc[p] = acc[p] + terms[i * probes : (i + 1) * probes, i * width : (i + 1) * width]
        return carry

    lax.fori_loop(0, (n + CHUNK - 1) // CHUNK, step, 0)
    out_ref[...] = acc[...].astype(out_ref.dtype)


def on_device(omega, jac_blocks, block_param, block_obs, block_count, obs_weight):
    probes = omega.shape[0]
    slots, width = jac_blocks.shape[1], jac_blocks.shape[2]
    pblocks = omega.shape[1] // width
    oblocks = obs_weight.shape[1] // width
    nz, nyh, ncore = (lax.axis_size(a) for a in PAR)
    smem = pl.BlockSpec(memory_space=pltpu.SMEM)
    vmem = pl.BlockSpec(memory_space=pltpu.VMEM)
    hbm = pl.BlockSpec(memory_space=pltpu.HBM)
    little = pltpu.CompilerParams(vmem_limit_bytes=8 << 20)
    params = pltpu.CompilerParams(vmem_limit_bytes=24 << 20)
    held = [
        pltpu.with_memory_space_constraint(a, pltpu.HBM)
        for a in (block_param, block_obs, omega, jac_blocks)
    ]
    rows = oblocks // ncore * probes
    each = oblocks // (nz * nyh * ncore) * probes
    per = each // probes
    quarter = lax.axis_index("core") * nyh + lax.axis_index("yh")
    weight = lax.dynamic_slice(
        obs_weight.reshape(oblocks, 1, width),
        ((quarter * nz + lax.axis_index("z")) * per, 0, 0),
        (per, 1, width),
    )
    sums, jac, bp, bo = pl.pallas_call(
        fwd_kernel,
        out_shape=(
            jax.ShapeDtypeStruct((ncore, rows + SUB, width), jnp.float32),
            jax.ShapeDtypeStruct((slots, width, width), jac_blocks.dtype),
            jax.ShapeDtypeStruct(block_param.shape, jnp.int32),
            jax.ShapeDtypeStruct(block_obs.shape, jnp.int32),
        ),
        in_specs=[smem] * 2 + [hbm] * 4,
        out_specs=(vmem, vmem, smem, smem),
        scratch_shapes=[
            pltpu.VMEM(omega.shape, omega.dtype),
            pltpu.SemaphoreType.DMA((3,)),
            pltpu.SemaphoreType.DMA((slots // CHUNK,)),
        ],
        compiler_params=params,
        name="fwd_blocks",
    )(quarter.reshape(1, 1), block_count, *held)
    sums, weight = lax.optimization_barrier((sums, weight))

    swap = [(i, 1 - i) for i in range(2)]
    mine, other = pl.pallas_call(
        core_kernel,
        out_shape=(
            jax.ShapeDtypeStruct((rows // nyh, width), jnp.float32),
            jax.ShapeDtypeStruct((rows // nyh + SUB, width), jnp.float32),
        ),
        in_specs=[vmem] * 2,
        out_specs=(vmem, vmem),
        compiler_params=little,
        name="add_core",
    )(sums, lax.ppermute(sums[1], "core", swap))
    got = lax.ppermute(other.astype(jnp.float16), "yh", swap).astype(jnp.float32)
    packed = pl.pallas_call(
        chip_kernel,
        out_shape=jax.ShapeDtypeStruct((nz, each + SUB, width), jnp.float32),
        in_specs=[vmem] * 3,
        out_specs=vmem,
        compiler_params=little,
        name="add_chip",
    )(mine, other, got)
    got = lax.all_to_all(packed.astype(jnp.float16), "z", 0, 0, tiled=True)
    scale = jnp.exp2(got[:, each:].astype(jnp.float32))
    data = got[:, :each].astype(jnp.float32).reshape(nz, each // SUB, SUB, width)
    owned = jnp.sum(data * scale[:, None], axis=0).reshape(per, probes, width)

    scaled = (owned * weight).astype(jnp.bfloat16)
    scaled = jnp.broadcast_to(scaled, (nz, per, probes, width)).reshape(nz * per, probes, width)
    scaled = lax.all_to_all(scaled, "z", 0, 0, tiled=True)
    scaled = lax.all_gather(scaled, "yh", axis=0, tiled=True)
    scaled = lax.all_gather(scaled, "core", axis=0, tiled=True)

    local_terms = pl.pallas_call(
        bwd_kernel,
        out_shape=jax.ShapeDtypeStruct((pblocks, probes, width), jnp.bfloat16),
        in_specs=[smem, smem, smem, vmem, vmem],
        out_specs=vmem,
        scratch_shapes=[pltpu.VMEM((pblocks, probes, width), jnp.float32)],
        compiler_params=params,
        name="bwd_blocks",
    )(block_count, bp, bo, scaled, jac)

    n = lax.axis_size(GRP)
    got = lax.all_to_all(local_terms, GRP, 0, 0, tiled=True)
    got = got.reshape(n, pblocks // n, probes, width).astype(jnp.float32)
    total = jnp.sum(got, axis=0)
    return jnp.transpose(total, (1, 0, 2)).reshape(probes, pblocks // n * width)


def solution(mesh):
    mesh = Mesh(mesh.devices.reshape(4, 2, 16, 2, 2), GRP + PAR)
    in_specs = (
        P(None, PAR),
        P(GRP, PAR, None, None),
        P(GRP, PAR),
        P(GRP, PAR),
        P(GRP, PAR),
        P(GRP, None),
    )
    out_specs = P(None, PAR + GRP)
    return jax.shard_map(
        on_device, mesh=mesh, in_specs=in_specs, out_specs=out_specs, check_vma=False
    )
```

```python
import jax
import jax.numpy as jnp
from jax import lax
from jax.experimental import pallas as pl
from jax.experimental.pallas import tpu as pltpu
from jax.sharding import Mesh, PartitionSpec as P

CHUNK = 64
SUB = 8
PAR = ("zh", "zl", "yh", "core")
NEAR = ("zl", "yh")
GRP = ("x", "yl")


def fwd_kernel(
    me, cnt, bp_hbm, bo_hbm, omega_hbm, jac_hbm, sums_ref, jac, bp, bo, omega, sems, jsems
):
    width = jac.shape[1]
    probes = omega.shape[0]
    rows = sums_ref.shape[1] - SUB
    half = rows // probes
    small = [
        pltpu.make_async_copy(src, dst, sems.at[i])
        for i, (src, dst) in enumerate(((bp_hbm, bp), (bo_hbm, bo), (omega_hbm, omega)))
    ]
    for copy in small:
        copy.start()
    n = cnt[0, 0]

    def chunk(c):
        at = pl.ds(pl.multiple_of(c * CHUNK, CHUNK), CHUNK)
        return pltpu.make_async_copy(jac_hbm.at[0, at], jac.at[at], jsems.at[c])

    for c in range(jac.shape[0] // CHUNK):

        @pl.when(c * CHUNK < n)
        def _():
            chunk(c).start()

    sums_ref[...] = jnp.zeros_like(sums_ref)
    flip = me[0, 0] * half
    for copy in small:
        copy.wait()

    def step(c, carry):
        chunk(c).wait()
        for j in range(CHUNK):
            s = c * CHUNK + j
            at = pl.multiple_of(bp[0, s] * width, width)
            panel = omega[:, pl.ds(at, width)]
            panel = jnp.where(s < n, panel, jnp.zeros_like(panel))
            term = jnp.dot(panel, jac[s], preferred_element_type=jnp.float32)
            o = bo[0, s] ^ flip
            at = pl.ds(pl.multiple_of(o % half * probes, probes), probes)
            sums_ref[o // half, at] = sums_ref[o // half, at] + term
        return carry

    lax.fori_loop(0, (n + CHUNK - 1) // CHUNK, step, 0)
    top = jnp.zeros((SUB, width), jnp.float32)
    for i in range(2):
        top = jnp.maximum(top, jnp.max(jnp.abs(sums_ref[i, :rows].reshape(rows // SUB, SUB, width)), axis=0))
    for i in range(2):
        sums_ref[i, rows:] = top


def exponent(top):
    return jnp.clip(jnp.ceil(jnp.log2(top)), -100.0, 100.0) - 14.0


def unscaled_sum(got_ref):
    parts, each, width = got_ref.shape
    each = each - SUB
    total = None
    for i in range(parts):
        data = got_ref[i, :each].reshape(each // SUB, SUB, width) * jnp.exp2(got_ref[i, each:])
        total = data if total is None else total + data
    return total


def core_kernel(sums_ref, got_ref, out_ref):
    parts, each, width = out_ref.shape
    each = each - SUB
    rows = parts * each
    power = exponent(sums_ref[0, rows:] + got_ref[rows:])
    data = (sums_ref[0, :rows] + got_ref[:rows]).reshape(rows // SUB, SUB, width) * jnp.exp2(-power)
    out_ref[:, :each] = data.reshape(parts, each, width)
    out_ref[:, each:] = jnp.broadcast_to(power, (parts, SUB, width))


def near_kernel(got_ref, out_ref):
    rows, width = out_ref.shape
    rows = rows - SUB
    total = unscaled_sum(got_ref)
    power = exponent(jnp.max(jnp.abs(total), axis=0))
    out_ref[:rows] = (total * jnp.exp2(-power)).reshape(rows, width)
    out_ref[rows:] = power


def far_kernel(got_ref, weight_ref, out_ref):
    copies, rows, width = out_ref.shape
    per = weight_ref.shape[0]
    total = unscaled_sum(got_ref).reshape(per, rows // per, width)
    scaled = (total * weight_ref[...]).reshape(rows, width).astype(out_ref.dtype)
    out_ref[...] = jnp.broadcast_to(scaled, (copies, rows, width))


def bwd_kernel(cnt, bp, bo, v_ref, jac, out_ref, acc):
    width = jac.shape[1]
    probes = v_ref.shape[1]
    n = cnt[0, 0]
    acc[...] = jnp.zeros_like(acc)

    def step(c, carry):
        for j in range(0, CHUNK, 2):
            first = c * CHUNK + j
            pair = []
            for s in (first, first + 1):
                v = v_ref[bo[0, s]]
                pair.append(jnp.where(s < n, v, jnp.zeros_like(v)))
            blocks = jac[pl.ds(first, 2)].reshape(2 * width, width)
            terms = lax.dot_general(
                jnp.concatenate(pair, axis=0),
                blocks,
                (((1,), (1,)), ((), ())),
                preferred_element_type=jnp.float32,
            )
            for i in range(2):
                p = bp[0, first + i]
                acc[p] = acc[p] + terms[i * probes : (i + 1) * probes, i * width : (i + 1) * width]
        return carry

    lax.fori_loop(0, (n + CHUNK - 1) // CHUNK, step, 0)
    out_ref[...] = acc[...].astype(out_ref.dtype)


def on_device(omega, jac_blocks, block_param, block_obs, block_count, obs_weight):
    probes = omega.shape[0]
    slots, width = jac_blocks.shape[1], jac_blocks.shape[2]
    pblocks = omega.shape[1] // width
    oblocks = obs_weight.shape[1] // width
    ncore, nnear = lax.axis_size("core"), lax.axis_size(NEAR)
    smem = pl.BlockSpec(memory_space=pltpu.SMEM)
    vmem = pl.BlockSpec(memory_space=pltpu.VMEM)
    hbm = pl.BlockSpec(memory_space=pltpu.HBM)
    little = pltpu.CompilerParams(vmem_limit_bytes=8 << 20)
    params = pltpu.CompilerParams(vmem_limit_bytes=24 << 20)
    held = [
        pltpu.with_memory_space_constraint(a, pltpu.HBM)
        for a in (block_param, block_obs, omega, jac_blocks)
    ]
    rows = oblocks // ncore * probes
    each = rows // nnear
    per = each // probes
    first = (lax.axis_index("core") * nnear + lax.axis_index(NEAR)) * per
    weight = lax.dynamic_slice(obs_weight.reshape(oblocks, 1, width), (first, 0, 0), (per, 1, width))
    sums, jac, bp, bo = pl.pallas_call(
        fwd_kernel,
        out_shape=(
            jax.ShapeDtypeStruct((ncore, rows + SUB, width), jnp.float32),
            jax.ShapeDtypeStruct((slots, width, width), jac_blocks.dtype),
            jax.ShapeDtypeStruct(block_param.shape, jnp.int32),
            jax.ShapeDtypeStruct(block_obs.shape, jnp.int32),
        ),
        in_specs=[smem] * 2 + [hbm] * 4,
        out_specs=(vmem, vmem, smem, smem),
        scratch_shapes=[
            pltpu.VMEM(omega.shape, omega.dtype),
            pltpu.SemaphoreType.DMA((3,)),
            pltpu.SemaphoreType.DMA((slots // CHUNK,)),
        ],
        compiler_params=params,
        name="fwd_blocks",
    )(lax.axis_index("core").reshape(1, 1), block_count, *held)
    sums, weight = lax.optimization_barrier((sums, weight))

    def small_call(kernel, shape, dtype, name):
        return pl.pallas_call(
            kernel,
            out_shape=jax.ShapeDtypeStruct(shape, dtype),
            out_specs=vmem,
            compiler_params=little,
            name=name,
        )

    packed = small_call(core_kernel, (nnear, each + SUB, width), jnp.float32, "add_core")(
        sums, lax.ppermute(sums[1], "core", [(0, 1), (1, 0)])
    )
    got = lax.all_to_all(packed.astype(jnp.float16), NEAR, 0, 0, tiled=True).astype(jnp.float32)
    packed = small_call(near_kernel, (each + SUB, width), jnp.float32, "add_near")(got)
    got = lax.all_gather(packed.astype(jnp.float16), "zh").astype(jnp.float32)
    scaled = small_call(far_kernel, (nnear, each, width), jnp.bfloat16, "add_far")(got, weight)
    scaled = lax.all_to_all(scaled, NEAR, 0, 0, tiled=True).reshape(rows, width)
    scaled = lax.all_gather(scaled, "core", axis=0, tiled=True).reshape(oblocks, probes, width)

    local_terms = pl.pallas_call(
        bwd_kernel,
        out_shape=jax.ShapeDtypeStruct((pblocks, probes, width), jnp.bfloat16),
        in_specs=[smem, smem, smem, vmem, vmem],
        out_specs=vmem,
        scratch_shapes=[pltpu.VMEM((pblocks, probes, width), jnp.float32)],
        compiler_params=params,
        name="bwd_blocks",
    )(block_count, bp, bo, scaled, jac)

    n = lax.axis_size(GRP)
    got = lax.all_to_all(local_terms, GRP, 0, 0, tiled=True)
    got = got.reshape(n, pblocks // n, probes, width).astype(jnp.float32)
    total = jnp.sum(got, axis=0)
    return jnp.transpose(total, (1, 0, 2)).reshape(probes, pblocks // n * width)


def solution(mesh):
    mesh = Mesh(mesh.devices.reshape(4, 2, 4, 4, 2, 2), GRP + PAR)
    in_specs = (
        P(None, PAR),
        P(GRP, PAR, None, None),
        P(GRP, PAR),
        P(GRP, PAR),
        P(GRP, PAR),
        P(GRP, None),
    )
    out_specs = P(None, PAR + GRP)
    return jax.shard_map(
        on_device, mesh=mesh, in_specs=in_specs, out_specs=out_specs, check_vma=False
    )
```

```python
import jax
import jax.numpy as jnp
from jax import lax
from jax.experimental import pallas as pl
from jax.experimental.pallas import tpu as pltpu
from jax.sharding import Mesh, PartitionSpec as P

CHUNK = 64
SUB = 8
PAR = ("zh", "zl", "yh", "core")
NEAR = ("zl", "yh")
GRP = ("x", "yl")


def fwd_kernel(
    me, cnt, bp_hbm, bo_hbm, omega_hbm, jac_hbm, sums_ref, jac, bp, bo, omega, sems, jsems
):
    width = jac.shape[1]
    probes = omega.shape[0]
    rows = sums_ref.shape[1] - SUB
    half = rows // probes
    small = [
        pltpu.make_async_copy(src, dst, sems.at[i])
        for i, (src, dst) in enumerate(((bp_hbm, bp), (bo_hbm, bo), (omega_hbm, omega)))
    ]
    for copy in small:
        copy.start()
    n = cnt[0, 0]

    def chunk(c):
        at = pl.ds(pl.multiple_of(c * CHUNK, CHUNK), CHUNK)
        return pltpu.make_async_copy(jac_hbm.at[0, at], jac.at[at], jsems.at[c])

    for c in range(jac.shape[0] // CHUNK):

        @pl.when(c * CHUNK < n)
        def _():
            chunk(c).start()

    sums_ref[...] = jnp.zeros_like(sums_ref)
    flip = me[0, 0] * half
    for copy in small:
        copy.wait()

    def step(c, carry):
        chunk(c).wait()
        for j in range(CHUNK):
            s = c * CHUNK + j
            at = pl.multiple_of(bp[0, s] * width, width)
            panel = omega[:, pl.ds(at, width)]
            panel = jnp.where(s < n, panel, jnp.zeros_like(panel))
            term = jnp.dot(panel, jac[s], preferred_element_type=jnp.float32)
            o = bo[0, s] ^ flip
            at = pl.ds(pl.multiple_of(o % half * probes, probes), probes)
            sums_ref[o // half, at] = sums_ref[o // half, at] + term
        return carry

    lax.fori_loop(0, (n + CHUNK - 1) // CHUNK, step, 0)
    top = jnp.zeros((SUB, width), jnp.float32)
    for i in range(2):
        top = jnp.maximum(top, jnp.max(jnp.abs(sums_ref[i, :rows].reshape(rows // SUB, SUB, width)), axis=0))
    for i in range(2):
        sums_ref[i, rows:] = top


def exponent(top):
    return jnp.clip(jnp.ceil(jnp.log2(top)), -100.0, 100.0) - 14.0


def unscaled_sum(got_ref):
    parts, each, width = got_ref.shape
    each = each - SUB
    total = None
    for i in range(parts):
        data = got_ref[i, :each].reshape(each // SUB, SUB, width) * jnp.exp2(got_ref[i, each:])
        total = data if total is None else total + data
    return total


def core_kernel(sums_ref, got_ref, out_ref):
    parts, each, width = out_ref.shape
    each = each - SUB
    rows = parts * each
    power = exponent(sums_ref[0, rows:] + got_ref[rows:])
    data = (sums_ref[0, :rows] + got_ref[:rows]).reshape(rows // SUB, SUB, width) * jnp.exp2(-power)
    out_ref[:, :each] = data.reshape(parts, each, width)
    out_ref[:, each:] = jnp.broadcast_to(power, (parts, SUB, width))


def near_kernel(got_ref, out_ref):
    rows, width = out_ref.shape
    rows = rows - SUB
    total = unscaled_sum(got_ref)
    power = exponent(jnp.max(jnp.abs(total), axis=0))
    out_ref[:rows] = (total * jnp.exp2(-power)).reshape(rows, width)
    out_ref[rows:] = power


def far_kernel(got_ref, weight_ref, out_ref):
    copies, rows, width = out_ref.shape
    per = weight_ref.shape[0]
    total = unscaled_sum(got_ref).reshape(per, rows // per, width)
    scaled = (total * weight_ref[...]).reshape(rows, width).astype(out_ref.dtype)
    out_ref[...] = jnp.broadcast_to(scaled, (copies, rows, width))


def bwd_kernel(cnt, bp, bo, v_ref, jac, out_ref, acc):
    width = jac.shape[1]
    probes = v_ref.shape[1]
    n = cnt[0, 0]
    acc[...] = jnp.zeros_like(acc)

    def step(c, carry):
        for j in range(0, CHUNK, 2):
            first = c * CHUNK + j
            pair = []
            for s in (first, first + 1):
                v = v_ref[bo[0, s]]
                pair.append(jnp.where(s < n, v, jnp.zeros_like(v)))
            blocks = jac[pl.ds(first, 2)].reshape(2 * width, width)
            terms = lax.dot_general(
                jnp.concatenate(pair, axis=0),
                blocks,
                (((1,), (1,)), ((), ())),
                preferred_element_type=jnp.float32,
            )
            for i in range(2):
                p = bp[0, first + i]
                acc[p] = acc[p] + terms[i * probes : (i + 1) * probes, i * width : (i + 1) * width]
        return carry

    lax.fori_loop(0, (n + CHUNK - 1) // CHUNK, step, 0)
    out_ref[...] = acc[...].astype(out_ref.dtype)


def on_device(omega, jac_blocks, block_param, block_obs, block_count, obs_weight):
    probes = omega.shape[0]
    slots, width = jac_blocks.shape[1], jac_blocks.shape[2]
    pblocks = omega.shape[1] // width
    oblocks = obs_weight.shape[1] // width
    ncore, nnear = lax.axis_size("core"), lax.axis_size(NEAR)
    smem = pl.BlockSpec(memory_space=pltpu.SMEM)
    vmem = pl.BlockSpec(memory_space=pltpu.VMEM)
    hbm = pl.BlockSpec(memory_space=pltpu.HBM)
    little = pltpu.CompilerParams(vmem_limit_bytes=8 << 20)
    params = pltpu.CompilerParams(vmem_limit_bytes=24 << 20)
    held = [
        pltpu.with_memory_space_constraint(a, pltpu.HBM)
        for a in (block_param, block_obs, omega, jac_blocks)
    ]
    rows = oblocks // ncore * probes
    each = rows // nnear
    per = each // probes
    first = (lax.axis_index("core") * nnear + lax.axis_index(NEAR)) * per
    weight = lax.dynamic_slice(obs_weight.reshape(oblocks, 1, width), (first, 0, 0), (per, 1, width))
    sums, jac, bp, bo = pl.pallas_call(
        fwd_kernel,
        out_shape=(
            jax.ShapeDtypeStruct((ncore, rows + SUB, width), jnp.float32),
            jax.ShapeDtypeStruct((slots, width, width), jac_blocks.dtype),
            jax.ShapeDtypeStruct(block_param.shape, jnp.int32),
            jax.ShapeDtypeStruct(block_obs.shape, jnp.int32),
        ),
        in_specs=[smem] * 2 + [hbm] * 4,
        out_specs=(vmem, vmem, smem, smem),
        scratch_shapes=[
            pltpu.VMEM(omega.shape, omega.dtype),
            pltpu.SemaphoreType.DMA((3,)),
            pltpu.SemaphoreType.DMA((slots // CHUNK,)),
        ],
        compiler_params=params,
        name="fwd_blocks",
    )(lax.axis_index("core").reshape(1, 1), block_count, *held)
    sums, weight = lax.optimization_barrier((sums, weight))

    def small_call(kernel, shape, dtype, name):
        return pl.pallas_call(
            kernel,
            out_shape=jax.ShapeDtypeStruct(shape, dtype),
            out_specs=vmem,
            compiler_params=little,
            name=name,
        )

    packed = small_call(core_kernel, (nnear, each + SUB, width), jnp.float32, "add_core")(
        sums, lax.ppermute(sums[1], "core", [(0, 1), (1, 0)])
    )
    got = lax.all_to_all(packed.astype(jnp.float16), NEAR, 0, 0, tiled=True).astype(jnp.float32)
    packed = small_call(near_kernel, (each + SUB, width), jnp.float32, "add_near")(got)
    nfar = lax.axis_size("zh")
    copies = jnp.broadcast_to(packed.astype(jnp.float16), (nfar,) + packed.shape)
    got = lax.all_to_all(copies, "zh", 0, 0, tiled=True).astype(jnp.float32)
    scaled = small_call(far_kernel, (nnear, each, width), jnp.bfloat16, "add_far")(got, weight)
    scaled = lax.all_to_all(scaled, NEAR, 0, 0, tiled=True).reshape(rows, width)
    scaled = lax.all_gather(scaled, "core", axis=0, tiled=True).reshape(oblocks, probes, width)

    local_terms = pl.pallas_call(
        bwd_kernel,
        out_shape=jax.ShapeDtypeStruct((pblocks, probes, width), jnp.bfloat16),
        in_specs=[smem, smem, smem, vmem, vmem],
        out_specs=vmem,
        scratch_shapes=[pltpu.VMEM((pblocks, probes, width), jnp.float32)],
        compiler_params=params,
        name="bwd_blocks",
    )(block_count, bp, bo, scaled, jac)

    n = lax.axis_size(GRP)
    got = lax.all_to_all(local_terms, GRP, 0, 0, tiled=True)
    got = got.reshape(n, pblocks // n, probes, width).astype(jnp.float32)
    total = jnp.sum(got, axis=0)
    return jnp.transpose(total, (1, 0, 2)).reshape(probes, pblocks // n * width)


def solution(mesh):
    mesh = Mesh(mesh.devices.reshape(4, 2, 4, 4, 2, 2), GRP + PAR)
    in_specs = (
        P(None, PAR),
        P(GRP, PAR, None, None),
        P(GRP, PAR),
        P(GRP, PAR),
        P(GRP, PAR),
        P(GRP, None),
    )
    out_specs = P(None, PAR + GRP)
    return jax.shard_map(
        on_device, mesh=mesh, in_specs=in_specs, out_specs=out_specs, check_vma=False
    )
```

```python
import jax
import jax.numpy as jnp
from jax import lax
from jax.experimental import pallas as pl
from jax.experimental.pallas import tpu as pltpu
from jax.sharding import Mesh, PartitionSpec as P

CHUNK = 64
SUB = 8
PAR = ("zh", "zl", "yh", "core")
NEAR = ("zl", "yh")
GRP = ("x", "yl")


def exponent(top):
    return jnp.clip(jnp.ceil(jnp.log2(top)), -100.0, 100.0) - 14.0


def fwd_kernel(
    me, cnt, bp_hbm, bo_hbm, omega_hbm, jac_hbm, sums_ref, jac, bp, bo, omega, sems, jsems
):
    width = jac.shape[1]
    probes = omega.shape[0]
    rows = sums_ref.shape[1] - SUB
    half = rows // probes
    small = [
        pltpu.make_async_copy(src, dst, sems.at[i])
        for i, (src, dst) in enumerate(((bp_hbm, bp), (bo_hbm, bo), (omega_hbm, omega)))
    ]
    for copy in small:
        copy.start()
    n = cnt[0, 0]

    def chunk(c):
        at = pl.ds(pl.multiple_of(c * CHUNK, CHUNK), CHUNK)
        return pltpu.make_async_copy(jac_hbm.at[0, at], jac.at[at], jsems.at[c])

    for c in range(jac.shape[0] // CHUNK):

        @pl.when(c * CHUNK < n)
        def _():
            chunk(c).start()

    sums_ref[...] = jnp.zeros_like(sums_ref)
    flip = me[0, 0] * half
    for copy in small:
        copy.wait()

    def step(c, carry):
        chunk(c).wait()
        for j in range(CHUNK):
            s = c * CHUNK + j
            at = pl.multiple_of(bp[0, s] * width, width)
            panel = omega[:, pl.ds(at, width)]
            panel = jnp.where(s < n, panel, jnp.zeros_like(panel))
            term = jnp.dot(panel, jac[s], preferred_element_type=jnp.float32)
            o = bo[0, s] ^ flip
            at = pl.ds(pl.multiple_of(o % half * probes, probes), probes)
            sums_ref[o // half, at] = sums_ref[o // half, at] + term
        return carry

    lax.fori_loop(0, (n + CHUNK - 1) // CHUNK, step, 0)
    top = jnp.zeros((SUB, width), jnp.float32)
    for i in range(2):
        top = jnp.maximum(top, jnp.max(jnp.abs(sums_ref[i, :rows].reshape(rows // SUB, SUB, width)), axis=0))
    power = exponent(top)
    other = sums_ref[1, :rows].reshape(rows // SUB, SUB, width) * jnp.exp2(-power)
    sums_ref[1, :rows] = other.reshape(rows, width)
    sums_ref[0, rows:] = top
    sums_ref[1, rows:] = power


def unscaled_sum(got_ref):
    parts, each, width = got_ref.shape
    each = each - SUB
    total = None
    for i in range(parts):
        data = got_ref[i, :each].reshape(each // SUB, SUB, width) * jnp.exp2(got_ref[i, each:])
        total = data if total is None else total + data
    return total


def core_kernel(me, sums_ref, got_ref, out_ref):
    parts, each, width = out_ref.shape
    each = each - SUB
    rows = parts * each
    got = got_ref[1 - me[0, 0]]
    theirs = got[rows:]
    power = exponent(sums_ref[0, rows:] + jnp.exp2(theirs + 14.0))
    data = sums_ref[0, :rows].reshape(rows // SUB, SUB, width) * jnp.exp2(-power)
    data = data + got[:rows].reshape(rows // SUB, SUB, width) * jnp.exp2(theirs - power)
    out_ref[:, :each] = data.reshape(parts, each, width)
    out_ref[:, each:] = jnp.broadcast_to(power, (parts, SUB, width))


def near_kernel(got_ref, out_ref):
    rows, width = out_ref.shape
    rows = rows - SUB
    total = unscaled_sum(got_ref)
    power = exponent(jnp.max(jnp.abs(total), axis=0))
    out_ref[:rows] = (total * jnp.exp2(-power)).reshape(rows, width)
    out_ref[rows:] = power


def far_kernel(got_ref, weight_ref, out_ref):
    copies, rows, width = out_ref.shape
    per = weight_ref.shape[0]
    total = unscaled_sum(got_ref).reshape(per, rows // per, width)
    scaled = (total * weight_ref[...]).reshape(rows, width).astype(out_ref.dtype)
    out_ref[...] = jnp.broadcast_to(scaled, (copies, rows, width))


def bwd_kernel(cnt, bp, bo, v_ref, jac, out_ref, acc):
    width = jac.shape[1]
    probes = v_ref.shape[1]
    n = cnt[0, 0]
    acc[...] = jnp.zeros_like(acc)

    def step(c, carry):
        for j in range(0, CHUNK, 2):
            first = c * CHUNK + j
            pair = []
            for s in (first, first + 1):
                v = v_ref[bo[0, s]]
                pair.append(jnp.where(s < n, v, jnp.zeros_like(v)))
            blocks = jac[pl.ds(first, 2)].reshape(2 * width, width)
            terms = lax.dot_general(
                jnp.concatenate(pair, axis=0),
                blocks,
                (((1,), (1,)), ((), ())),
                preferred_element_type=jnp.float32,
            )
            for i in range(2):
                p = bp[0, first + i]
                acc[p] = acc[p] + terms[i * probes : (i + 1) * probes, i * width : (i + 1) * width]
        return carry

    lax.fori_loop(0, (n + CHUNK - 1) // CHUNK, step, 0)
    out_ref[...] = acc[...].astype(out_ref.dtype)


def on_device(omega, jac_blocks, block_param, block_obs, block_count, obs_weight):
    probes = omega.shape[0]
    slots, width = jac_blocks.shape[1], jac_blocks.shape[2]
    pblocks = omega.shape[1] // width
    oblocks = obs_weight.shape[1] // width
    ncore, nnear = lax.axis_size("core"), lax.axis_size(NEAR)
    smem = pl.BlockSpec(memory_space=pltpu.SMEM)
    vmem = pl.BlockSpec(memory_space=pltpu.VMEM)
    hbm = pl.BlockSpec(memory_space=pltpu.HBM)
    little = pltpu.CompilerParams(vmem_limit_bytes=8 << 20)
    params = pltpu.CompilerParams(vmem_limit_bytes=24 << 20)
    held = [
        pltpu.with_memory_space_constraint(a, pltpu.HBM)
        for a in (block_param, block_obs, omega, jac_blocks)
    ]
    rows = oblocks // ncore * probes
    each = rows // nnear
    per = each // probes
    me = lax.axis_index("core").reshape(1, 1)
    first = (lax.axis_index("core") * nnear + lax.axis_index(NEAR)) * per
    weight = lax.dynamic_slice(obs_weight.reshape(oblocks, 1, width), (first, 0, 0), (per, 1, width))
    sums, jac, bp, bo = pl.pallas_call(
        fwd_kernel,
        out_shape=(
            jax.ShapeDtypeStruct((ncore, rows + SUB, width), jnp.float32),
            jax.ShapeDtypeStruct((slots, width, width), jac_blocks.dtype),
            jax.ShapeDtypeStruct(block_param.shape, jnp.int32),
            jax.ShapeDtypeStruct(block_obs.shape, jnp.int32),
        ),
        in_specs=[smem] * 2 + [hbm] * 4,
        out_specs=(vmem, vmem, smem, smem),
        scratch_shapes=[
            pltpu.VMEM(omega.shape, omega.dtype),
            pltpu.SemaphoreType.DMA((3,)),
            pltpu.SemaphoreType.DMA((slots // CHUNK,)),
        ],
        compiler_params=params,
        name="fwd_blocks",
    )(me, block_count, *held)
    sums, weight = lax.optimization_barrier((sums, weight))

    def small_call(kernel, shape, dtype, name, in_specs):
        return pl.pallas_call(
            kernel,
            out_shape=jax.ShapeDtypeStruct(shape, dtype),
            in_specs=in_specs,
            out_specs=vmem,
            compiler_params=little,
            name=name,
        )

    got = lax.all_gather(sums[1].astype(jnp.float16), "core").astype(jnp.float32)
    packed = small_call(
        core_kernel, (nnear, each + SUB, width), jnp.float32, "add_core", [smem, vmem, vmem]
    )(me, sums, got)
    got = lax.all_to_all(packed.astype(jnp.float16), NEAR, 0, 0, tiled=True).astype(jnp.float32)
    packed = small_call(near_kernel, (each + SUB, width), jnp.float32, "add_near", [vmem])(got)
    got = lax.all_gather(packed.astype(jnp.float16), "zh").astype(jnp.float32)
    scaled = small_call(far_kernel, (nnear, each, width), jnp.bfloat16, "add_far", [vmem] * 2)(got, weight)
    scaled = lax.all_to_all(scaled, NEAR, 0, 0, tiled=True).reshape(rows, width)
    scaled = lax.all_gather(scaled, "core", axis=0, tiled=True).reshape(oblocks, probes, width)

    local_terms = pl.pallas_call(
        bwd_kernel,
        out_shape=jax.ShapeDtypeStruct((pblocks, probes, width), jnp.bfloat16),
        in_specs=[smem, smem, smem, vmem, vmem],
        out_specs=vmem,
        scratch_shapes=[pltpu.VMEM((pblocks, probes, width), jnp.float32)],
        compiler_params=params,
        name="bwd_blocks",
    )(block_count, bp, bo, scaled, jac)

    n = lax.axis_size(GRP)
    got = lax.all_to_all(local_terms, GRP, 0, 0, tiled=True)
    got = got.reshape(n, pblocks // n, probes, width).astype(jnp.float32)
    total = jnp.sum(got, axis=0)
    return jnp.transpose(total, (1, 0, 2)).reshape(probes, pblocks // n * width)


def solution(mesh):
    mesh = Mesh(mesh.devices.reshape(4, 2, 4, 4, 2, 2), GRP + PAR)
    in_specs = (
        P(None, PAR),
        P(GRP, PAR, None, None),
        P(GRP, PAR),
        P(GRP, PAR),
        P(GRP, PAR),
        P(GRP, None),
    )
    out_specs = P(None, PAR + GRP)
    return jax.shard_map(
        on_device, mesh=mesh, in_specs=in_specs, out_specs=out_specs, check_vma=False
    )
```

```python
import jax
import jax.numpy as jnp
from jax import lax
from jax.experimental import pallas as pl
from jax.experimental.pallas import tpu as pltpu
from jax.sharding import Mesh, PartitionSpec as P

CHUNK = 64
GROUP = 4
SUB = 8
PAR = ("zh", "zl", "yh", "core")
NEAR = ("zl", "yh")
GRP = ("x", "yl")


def exponent(top):
    return jnp.clip(jnp.ceil(jnp.log2(top)), -100.0, 100.0) - 14.0


def fwd_kernel(
    me, cnt, bp_hbm, bo_hbm, omega_hbm, jac_hbm, sums_ref, jac, bp, bo, omega, sems, jsems
):
    width = jac.shape[1]
    probes = omega.shape[0]
    rows = sums_ref.shape[1] - SUB
    half = rows // probes
    small = [
        pltpu.make_async_copy(src, dst, sems.at[i])
        for i, (src, dst) in enumerate(((bp_hbm, bp), (bo_hbm, bo), (omega_hbm, omega)))
    ]
    for copy in small:
        copy.start()
    n = cnt[0, 0]

    def chunk(c):
        at = pl.ds(pl.multiple_of(c * CHUNK, CHUNK), CHUNK)
        return pltpu.make_async_copy(jac_hbm.at[0, at], jac.at[at], jsems.at[c])

    for c in range(jac.shape[0] // CHUNK):

        @pl.when(c * CHUNK < n)
        def _():
            chunk(c).start()

    sums_ref[...] = jnp.zeros_like(sums_ref)
    flip = me[0, 0] * half
    for copy in small:
        copy.wait()

    def step(c, carry):
        chunk(c).wait()
        for j in range(CHUNK):
            s = c * CHUNK + j
            at = pl.multiple_of(bp[0, s] * width, width)
            panel = omega[:, pl.ds(at, width)]
            panel = jnp.where(s < n, panel, jnp.zeros_like(panel))
            term = jnp.dot(panel, jac[s], preferred_element_type=jnp.float32)
            o = bo[0, s] ^ flip
            at = pl.ds(pl.multiple_of(o % half * probes, probes), probes)
            sums_ref[o // half, at] = sums_ref[o // half, at] + term
        return carry

    lax.fori_loop(0, (n + CHUNK - 1) // CHUNK, step, 0)
    top = jnp.zeros((SUB, width), jnp.float32)
    for i in range(2):
        top = jnp.maximum(top, jnp.max(jnp.abs(sums_ref[i, :rows].reshape(rows // SUB, SUB, width)), axis=0))
    power = exponent(top)
    other = sums_ref[1, :rows].reshape(rows // SUB, SUB, width) * jnp.exp2(-power)
    sums_ref[1, :rows] = other.reshape(rows, width)
    sums_ref[0, rows:] = top
    sums_ref[1, rows:] = power


def unscaled_sum(got_ref):
    parts, each, width = got_ref.shape
    each = each - SUB
    total = None
    for i in range(parts):
        data = got_ref[i, :each].reshape(each // SUB, SUB, width) * jnp.exp2(got_ref[i, each:])
        total = data if total is None else total + data
    return total


def core_kernel(me, sums_ref, got_ref, out_ref):
    parts, each, width = out_ref.shape
    each = each - SUB
    rows = parts * each
    got = got_ref[1 - me[0, 0]]
    theirs = got[rows:]
    power = exponent(sums_ref[0, rows:] + jnp.exp2(theirs + 14.0))
    data = sums_ref[0, :rows].reshape(rows // SUB, SUB, width) * jnp.exp2(-power)
    data = data + got[:rows].reshape(rows // SUB, SUB, width) * jnp.exp2(theirs - power)
    out_ref[:, :each] = data.reshape(parts, each, width)
    out_ref[:, each:] = jnp.broadcast_to(power, (parts, SUB, width))


def near_kernel(got_ref, out_ref):
    rows, width = out_ref.shape
    rows = rows - SUB
    total = unscaled_sum(got_ref)
    power = exponent(jnp.max(jnp.abs(total), axis=0))
    out_ref[:rows] = (total * jnp.exp2(-power)).reshape(rows, width)
    out_ref[rows:] = power


def far_kernel(got_ref, weight_ref, out_ref):
    copies, rows, width = out_ref.shape
    per = weight_ref.shape[0]
    total = unscaled_sum(got_ref).reshape(per, rows // per, width)
    scaled = (total * weight_ref[...]).reshape(rows, width).astype(out_ref.dtype)
    out_ref[...] = jnp.broadcast_to(scaled, (copies, rows, width))


def bwd_kernel(cnt, bp, bo, v_ref, jac, out_ref, acc):
    width = jac.shape[1]
    probes = v_ref.shape[1]
    n = cnt[0, 0]
    acc[...] = jnp.zeros_like(acc)

    def step(c, carry):
        for j in range(0, CHUNK, GROUP):
            first = c * CHUNK + j
            group = []
            for s in range(GROUP):
                s = first + s
                v = v_ref[bo[0, s]]
                group.append(jnp.where(s < n, v, jnp.zeros_like(v)))
            blocks = jac[pl.ds(first, GROUP)].reshape(GROUP * width, width)
            terms = lax.dot_general(
                jnp.concatenate(group, axis=0),
                blocks,
                (((1,), (1,)), ((), ())),
                preferred_element_type=jnp.float32,
            )
            for i in range(GROUP):
                p = bp[0, first + i]
                acc[p] = acc[p] + terms[i * probes : (i + 1) * probes, i * width : (i + 1) * width]
        return carry

    lax.fori_loop(0, (n + CHUNK - 1) // CHUNK, step, 0)
    out_ref[...] = acc[...].astype(out_ref.dtype)


def on_device(omega, jac_blocks, block_param, block_obs, block_count, obs_weight):
    probes = omega.shape[0]
    slots, width = jac_blocks.shape[1], jac_blocks.shape[2]
    pblocks = omega.shape[1] // width
    oblocks = obs_weight.shape[1] // width
    ncore, nnear = lax.axis_size("core"), lax.axis_size(NEAR)
    smem = pl.BlockSpec(memory_space=pltpu.SMEM)
    vmem = pl.BlockSpec(memory_space=pltpu.VMEM)
    hbm = pl.BlockSpec(memory_space=pltpu.HBM)
    little = pltpu.CompilerParams(vmem_limit_bytes=8 << 20)
    params = pltpu.CompilerParams(vmem_limit_bytes=24 << 20)
    held = [
        pltpu.with_memory_space_constraint(a, pltpu.HBM)
        for a in (block_param, block_obs, omega, jac_blocks)
    ]
    rows = oblocks // ncore * probes
    each = rows // nnear
    per = each // probes
    me = lax.axis_index("core").reshape(1, 1)
    first = (lax.axis_index("core") * nnear + lax.axis_index(NEAR)) * per
    weight = lax.dynamic_slice(obs_weight.reshape(oblocks, 1, width), (first, 0, 0), (per, 1, width))
    sums, jac = pl.pallas_call(
        fwd_kernel,
        out_shape=(
            jax.ShapeDtypeStruct((ncore, rows + SUB, width), jnp.float32),
            jax.ShapeDtypeStruct((slots, width, width), jac_blocks.dtype),
        ),
        in_specs=[smem] * 2 + [hbm] * 4,
        out_specs=(vmem, vmem),
        scratch_shapes=[
            pltpu.SMEM(block_param.shape, jnp.int32),
            pltpu.SMEM(block_obs.shape, jnp.int32),
            pltpu.VMEM(omega.shape, omega.dtype),
            pltpu.SemaphoreType.DMA((3,)),
            pltpu.SemaphoreType.DMA((slots // CHUNK,)),
        ],
        compiler_params=params,
        name="fwd_blocks",
    )(me, block_count, *held)
    sums, weight = lax.optimization_barrier((sums, weight))

    def small_call(kernel, shape, dtype, name, in_specs):
        return pl.pallas_call(
            kernel,
            out_shape=jax.ShapeDtypeStruct(shape, dtype),
            in_specs=in_specs,
            out_specs=vmem,
            compiler_params=little,
            name=name,
        )

    got = lax.all_gather(sums[1].astype(jnp.float16), "core").astype(jnp.float32)
    packed = small_call(
        core_kernel, (nnear, each + SUB, width), jnp.float32, "add_core", [smem, vmem, vmem]
    )(me, sums, got)
    got = lax.all_to_all(packed.astype(jnp.float16), NEAR, 0, 0, tiled=True).astype(jnp.float32)
    packed = small_call(near_kernel, (each + SUB, width), jnp.float32, "add_near", [vmem])(got)
    got = lax.all_gather(packed.astype(jnp.float16), "zh").astype(jnp.float32)
    scaled = small_call(far_kernel, (nnear, each, width), jnp.bfloat16, "add_far", [vmem] * 2)(got, weight)
    scaled = lax.all_to_all(scaled, NEAR, 0, 0, tiled=True).reshape(rows, width)
    scaled = lax.all_gather(scaled, "core", axis=0, tiled=True).reshape(oblocks, probes, width)

    local_terms = pl.pallas_call(
        bwd_kernel,
        out_shape=jax.ShapeDtypeStruct((pblocks, probes, width), jnp.bfloat16),
        in_specs=[smem, smem, smem, vmem, vmem],
        out_specs=vmem,
        scratch_shapes=[pltpu.VMEM((pblocks, probes, width), jnp.float32)],
        compiler_params=params,
        name="bwd_blocks",
    )(block_count, block_param, block_obs, scaled, jac)

    n = lax.axis_size(GRP)
    got = lax.all_to_all(local_terms, GRP, 0, 0, tiled=True)
    got = got.reshape(n, pblocks // n, probes, width).astype(jnp.float32)
    total = jnp.sum(got, axis=0)
    return jnp.transpose(total, (1, 0, 2)).reshape(probes, pblocks // n * width)


def solution(mesh):
    mesh = Mesh(mesh.devices.reshape(4, 2, 4, 4, 2, 2), GRP + PAR)
    in_specs = (
        P(None, PAR),
        P(GRP, PAR, None, None),
        P(GRP, PAR),
        P(GRP, PAR),
        P(GRP, PAR),
        P(GRP, None),
    )
    out_specs = P(None, PAR + GRP)
    return jax.shard_map(
        on_device, mesh=mesh, in_specs=in_specs, out_specs=out_specs, check_vma=False
    )
```

```python
import jax
import jax.numpy as jnp
from jax import lax
from jax.experimental import pallas as pl
from jax.experimental.pallas import tpu as pltpu
from jax.sharding import Mesh, PartitionSpec as P

CHUNK = 64
GROUP = 4
SUB = 8
PAR = ("zh", "zl", "yh", "core")
NEAR = ("zl", "yh")
GRP = ("x", "yl")


def exponent(top):
    return jnp.clip(jnp.ceil(jnp.log2(top)), -100.0, 100.0) - 14.0


def fwd_kernel(
    me, cnt, bp_hbm, bo_hbm, omega_hbm, jac_hbm, sums_ref, jac, bp, bo, omega, sems, jsems
):
    width = jac.shape[1]
    probes = omega.shape[0]
    rows = sums_ref.shape[1] - SUB
    half = rows // probes
    small = [
        pltpu.make_async_copy(src, dst, sems.at[i])
        for i, (src, dst) in enumerate(((bp_hbm, bp), (bo_hbm, bo), (omega_hbm, omega)))
    ]
    for copy in small:
        copy.start()
    n = cnt[0, 0]

    def chunk(c):
        at = pl.ds(pl.multiple_of(c * CHUNK, CHUNK), CHUNK)
        return pltpu.make_async_copy(jac_hbm.at[0, at], jac.at[at], jsems.at[c])

    for c in range(jac.shape[0] // CHUNK):

        @pl.when(c * CHUNK < n)
        def _():
            chunk(c).start()

    sums_ref[...] = jnp.zeros_like(sums_ref)
    flip = me[0, 0] * half
    for copy in small:
        copy.wait()

    def step(c, carry):
        chunk(c).wait()
        for j in range(CHUNK):
            s = c * CHUNK + j
            at = pl.multiple_of(bp[0, s] * width, width)
            panel = omega[:, pl.ds(at, width)]
            panel = jnp.where(s < n, panel, jnp.zeros_like(panel))
            term = jnp.dot(panel, jac[s], preferred_element_type=jnp.float32)
            o = bo[0, s] ^ flip
            at = pl.ds(pl.multiple_of(o % half * probes, probes), probes)
            sums_ref[o // half, at] = sums_ref[o // half, at] + term
        return carry

    lax.fori_loop(0, (n + CHUNK - 1) // CHUNK, step, 0)
    top = jnp.zeros((SUB, width), jnp.float32)
    for i in range(2):
        top = jnp.maximum(top, jnp.max(jnp.abs(sums_ref[i, :rows].reshape(rows // SUB, SUB, width)), axis=0))
    power = exponent(top)
    other = sums_ref[1, :rows].reshape(rows // SUB, SUB, width) * jnp.exp2(-power)
    sums_ref[1, :rows] = other.reshape(rows, width)
    sums_ref[0, rows:] = top
    sums_ref[1, rows:] = power


def unscaled_sum(got_ref):
    parts, each, width = got_ref.shape
    each = each - SUB
    total = None
    for i in range(parts):
        data = got_ref[i, :each].reshape(each // SUB, SUB, width) * jnp.exp2(got_ref[i, each:])
        total = data if total is None else total + data
    return total


def core_kernel(me, sums_ref, got_ref, out_ref):
    parts, each, width = out_ref.shape
    each = each - SUB
    rows = parts * each
    got = got_ref[1 - me[0, 0]]
    theirs = got[rows:]
    power = exponent(sums_ref[0, rows:] + jnp.exp2(theirs + 14.0))
    data = sums_ref[0, :rows].reshape(rows // SUB, SUB, width) * jnp.exp2(-power)
    data = data + got[:rows].reshape(rows // SUB, SUB, width) * jnp.exp2(theirs - power)
    out_ref[:, :each] = data.reshape(parts, each, width)
    out_ref[:, each:] = jnp.broadcast_to(power, (parts, SUB, width))


def near_kernel(got_ref, out_ref):
    rows, width = out_ref.shape
    rows = rows - SUB
    total = unscaled_sum(got_ref)
    power = exponent(jnp.max(jnp.abs(total), axis=0))
    out_ref[:rows] = (total * jnp.exp2(-power)).reshape(rows, width)
    out_ref[rows:] = power


def far_kernel(got_ref, weight_ref, out_ref):
    copies, rows, width = out_ref.shape
    per = weight_ref.shape[0]
    total = unscaled_sum(got_ref).reshape(per, rows // per, width)
    scaled = (total * weight_ref[...]).reshape(rows, width).astype(out_ref.dtype)
    out_ref[...] = jnp.broadcast_to(scaled, (copies, rows, width))


def total_kernel(got_ref, out_ref):
    parts, blocks, _, width = got_ref.shape
    for j in range(blocks):
        total = got_ref[0, j].astype(jnp.float32)
        for i in range(1, parts):
            total = total + got_ref[i, j].astype(jnp.float32)
        out_ref[:, j * width : (j + 1) * width] = total


def bwd_kernel(cnt, bp, bo, v_ref, jac, out_ref, acc):
    width = jac.shape[1]
    probes = v_ref.shape[1]
    n = cnt[0, 0]
    acc[...] = jnp.zeros_like(acc)

    def step(c, carry):
        for j in range(0, CHUNK, GROUP):
            first = c * CHUNK + j
            group = []
            for s in range(GROUP):
                s = first + s
                v = v_ref[bo[0, s]]
                group.append(jnp.where(s < n, v, jnp.zeros_like(v)))
            blocks = jac[pl.ds(first, GROUP)].reshape(GROUP * width, width)
            terms = lax.dot_general(
                jnp.concatenate(group, axis=0),
                blocks,
                (((1,), (1,)), ((), ())),
                preferred_element_type=jnp.float32,
            )
            for i in range(GROUP):
                p = bp[0, first + i]
                acc[p] = acc[p] + terms[i * probes : (i + 1) * probes, i * width : (i + 1) * width]
        return carry

    lax.fori_loop(0, (n + CHUNK - 1) // CHUNK, step, 0)
    out_ref[...] = acc[...].astype(out_ref.dtype)


def on_device(omega, jac_blocks, block_param, block_obs, block_count, obs_weight):
    probes = omega.shape[0]
    slots, width = jac_blocks.shape[1], jac_blocks.shape[2]
    pblocks = omega.shape[1] // width
    oblocks = obs_weight.shape[1] // width
    ncore, nnear = lax.axis_size("core"), lax.axis_size(NEAR)
    smem = pl.BlockSpec(memory_space=pltpu.SMEM)
    vmem = pl.BlockSpec(memory_space=pltpu.VMEM)
    hbm = pl.BlockSpec(memory_space=pltpu.HBM)
    little = pltpu.CompilerParams(vmem_limit_bytes=8 << 20)
    params = pltpu.CompilerParams(vmem_limit_bytes=24 << 20)
    held = [
        pltpu.with_memory_space_constraint(a, pltpu.HBM)
        for a in (block_param, block_obs, omega, jac_blocks)
    ]
    rows = oblocks // ncore * probes
    each = rows // nnear
    per = each // probes
    me = lax.axis_index("core").reshape(1, 1)
    first = (lax.axis_index("core") * nnear + lax.axis_index(NEAR)) * per
    weight = lax.dynamic_slice(obs_weight.reshape(oblocks, 1, width), (first, 0, 0), (per, 1, width))
    sums, jac = pl.pallas_call(
        fwd_kernel,
        out_shape=(
            jax.ShapeDtypeStruct((ncore, rows + SUB, width), jnp.float32),
            jax.ShapeDtypeStruct((slots, width, width), jac_blocks.dtype),
        ),
        in_specs=[smem] * 2 + [hbm] * 4,
        out_specs=(vmem, vmem),
        scratch_shapes=[
            pltpu.SMEM(block_param.shape, jnp.int32),
            pltpu.SMEM(block_obs.shape, jnp.int32),
            pltpu.VMEM(omega.shape, omega.dtype),
            pltpu.SemaphoreType.DMA((3,)),
            pltpu.SemaphoreType.DMA((slots // CHUNK,)),
        ],
        compiler_params=params,
        name="fwd_blocks",
    )(me, block_count, *held)
    sums, weight = lax.optimization_barrier((sums, weight))

    def small_call(kernel, shape, dtype, name, in_specs):
        return pl.pallas_call(
            kernel,
            out_shape=jax.ShapeDtypeStruct(shape, dtype),
            in_specs=in_specs,
            out_specs=vmem,
            compiler_params=little,
            name=name,
        )

    got = lax.all_gather(sums[1].astype(jnp.float16), "core").astype(jnp.float32)
    packed = small_call(
        core_kernel, (nnear, each + SUB, width), jnp.float32, "add_core", [smem, vmem, vmem]
    )(me, sums, got)
    got = lax.all_to_all(packed.astype(jnp.float16), NEAR, 0, 0, tiled=True).astype(jnp.float32)
    packed = small_call(near_kernel, (each + SUB, width), jnp.float32, "add_near", [vmem])(got)
    got = lax.all_gather(packed.astype(jnp.float16), "zh").astype(jnp.float32)
    scaled = small_call(far_kernel, (nnear, each, width), jnp.bfloat16, "add_far", [vmem] * 2)(got, weight)
    scaled = lax.all_to_all(scaled, NEAR, 0, 0, tiled=True).reshape(rows, width)
    scaled = lax.all_gather(scaled, "core", axis=0, tiled=True).reshape(oblocks, probes, width)

    local_terms = pl.pallas_call(
        bwd_kernel,
        out_shape=jax.ShapeDtypeStruct((pblocks, probes, width), jnp.bfloat16),
        in_specs=[smem, smem, smem, vmem, vmem],
        out_specs=vmem,
        scratch_shapes=[pltpu.VMEM((pblocks, probes, width), jnp.float32)],
        compiler_params=params,
        name="bwd_blocks",
    )(block_count, block_param, block_obs, scaled, jac)

    n = lax.axis_size(GRP)
    got = lax.all_to_all(local_terms, GRP, 0, 0, tiled=True)
    got = got.reshape(n, pblocks // n, probes, width)
    return small_call(
        total_kernel, (probes, pblocks // n * width), jnp.float32, "add_groups", [vmem]
    )(got)


def solution(mesh):
    mesh = Mesh(mesh.devices.reshape(4, 2, 4, 4, 2, 2), GRP + PAR)
    in_specs = (
        P(None, PAR),
        P(GRP, PAR, None, None),
        P(GRP, PAR),
        P(GRP, PAR),
        P(GRP, PAR),
        P(GRP, None),
    )
    out_specs = P(None, PAR + GRP)
    return jax.shard_map(
        on_device, mesh=mesh, in_specs=in_specs, out_specs=out_specs, check_vma=False
    )
```

```python
import jax
import jax.numpy as jnp
from jax import lax
from jax.experimental import pallas as pl
from jax.experimental.pallas import tpu as pltpu
from jax.sharding import Mesh, PartitionSpec as P

CHUNK = 64
PIECES = ((0, 64), (64, 32), (96, 32))
GROUP = 4
SUB = 8
PAR = ("zh", "zl", "yh", "core")
NEAR = ("zl", "yh")
GRP = ("x", "yl")


def exponent(top):
    return jnp.clip(jnp.ceil(jnp.log2(top)), -100.0, 100.0) - 14.0


def fwd_kernel(
    me, cnt, bp_hbm, bo_hbm, omega_hbm, jac_hbm, sums_ref, jac, bp, bo, omega, sems, jsems
):
    width = jac.shape[1]
    probes = omega.shape[0]
    rows = sums_ref.shape[1] - SUB
    half = rows // probes
    small = [
        pltpu.make_async_copy(src, dst, sems.at[i])
        for i, (src, dst) in enumerate(((bp_hbm, bp), (bo_hbm, bo), (omega_hbm, omega)))
    ]
    for copy in small:
        copy.start()
    n = cnt[0, 0]

    def piece(i):
        at = pl.ds(*PIECES[i])
        return pltpu.make_async_copy(jac_hbm.at[0, at], jac.at[at], jsems.at[i])

    piece(0).start()

    @pl.when(n > CHUNK)
    def _():
        for i in range(1, len(PIECES)):
            piece(i).start()

    sums_ref[...] = jnp.zeros_like(sums_ref)
    flip = me[0, 0] * half
    for copy in small:
        copy.wait()

    def use(i):
        piece(i).wait()
        for s in range(PIECES[i][0], sum(PIECES[i])):
            at = pl.multiple_of(bp[0, s] * width, width)
            panel = omega[:, pl.ds(at, width)]
            panel = jnp.where(s < n, panel, jnp.zeros_like(panel))
            term = jnp.dot(panel, jac[s], preferred_element_type=jnp.float32)
            o = bo[0, s] ^ flip
            at = pl.ds(pl.multiple_of(o % half * probes, probes), probes)
            sums_ref[o // half, at] = sums_ref[o // half, at] + term

    use(0)

    @pl.when(n > CHUNK)
    def _():
        for i in range(1, len(PIECES)):
            use(i)

    top = jnp.zeros((SUB, width), jnp.float32)
    for i in range(2):
        top = jnp.maximum(top, jnp.max(jnp.abs(sums_ref[i, :rows].reshape(rows // SUB, SUB, width)), axis=0))
    power = exponent(top)
    other = sums_ref[1, :rows].reshape(rows // SUB, SUB, width) * jnp.exp2(-power)
    sums_ref[1, :rows] = other.reshape(rows, width)
    sums_ref[0, rows:] = top
    sums_ref[1, rows:] = power


def unscaled_sum(got_ref):
    parts, each, width = got_ref.shape
    each = each - SUB
    total = None
    for i in range(parts):
        data = got_ref[i, :each].reshape(each // SUB, SUB, width) * jnp.exp2(got_ref[i, each:])
        total = data if total is None else total + data
    return total


def core_kernel(me, sums_ref, got_ref, out_ref):
    parts, each, width = out_ref.shape
    each = each - SUB
    rows = parts * each
    got = got_ref[1 - me[0, 0]]
    theirs = got[rows:]
    power = exponent(sums_ref[0, rows:] + jnp.exp2(theirs + 14.0))
    data = sums_ref[0, :rows].reshape(rows // SUB, SUB, width) * jnp.exp2(-power)
    data = data + got[:rows].reshape(rows // SUB, SUB, width) * jnp.exp2(theirs - power)
    out_ref[:, :each] = data.reshape(parts, each, width)
    out_ref[:, each:] = jnp.broadcast_to(power, (parts, SUB, width))


def near_kernel(got_ref, out_ref):
    rows, width = out_ref.shape
    rows = rows - SUB
    total = unscaled_sum(got_ref)
    power = exponent(jnp.max(jnp.abs(total), axis=0))
    out_ref[:rows] = (total * jnp.exp2(-power)).reshape(rows, width)
    out_ref[rows:] = power


def far_kernel(got_ref, weight_ref, out_ref):
    copies, rows, width = out_ref.shape
    per = weight_ref.shape[0]
    total = unscaled_sum(got_ref).reshape(per, rows // per, width)
    scaled = (total * weight_ref[...]).reshape(rows, width).astype(out_ref.dtype)
    out_ref[...] = jnp.broadcast_to(scaled, (copies, rows, width))


def total_kernel(got_ref, out_ref):
    parts, blocks, _, width = got_ref.shape
    for j in range(blocks):
        total = got_ref[0, j].astype(jnp.float32)
        for i in range(1, parts):
            total = total + got_ref[i, j].astype(jnp.float32)
        out_ref[:, j * width : (j + 1) * width] = total


def bwd_kernel(cnt, bp, bo, v_ref, jac, out_ref, acc):
    width = jac.shape[1]
    probes = v_ref.shape[1]
    n = cnt[0, 0]
    acc[...] = jnp.zeros_like(acc)

    def step(c, carry):
        for j in range(0, CHUNK, GROUP):
            first = c * CHUNK + j
            group = []
            for s in range(GROUP):
                s = first + s
                v = v_ref[bo[0, s]]
                group.append(jnp.where(s < n, v, jnp.zeros_like(v)))
            blocks = jac[pl.ds(first, GROUP)].reshape(GROUP * width, width)
            terms = lax.dot_general(
                jnp.concatenate(group, axis=0),
                blocks,
                (((1,), (1,)), ((), ())),
                preferred_element_type=jnp.float32,
            )
            for i in range(GROUP):
                p = bp[0, first + i]
                acc[p] = acc[p] + terms[i * probes : (i + 1) * probes, i * width : (i + 1) * width]
        return carry

    lax.fori_loop(0, (n + CHUNK - 1) // CHUNK, step, 0)
    out_ref[...] = acc[...].astype(out_ref.dtype)


def on_device(omega, jac_blocks, block_param, block_obs, block_count, obs_weight):
    probes = omega.shape[0]
    slots, width = jac_blocks.shape[1], jac_blocks.shape[2]
    pblocks = omega.shape[1] // width
    oblocks = obs_weight.shape[1] // width
    ncore, nnear = lax.axis_size("core"), lax.axis_size(NEAR)
    smem = pl.BlockSpec(memory_space=pltpu.SMEM)
    vmem = pl.BlockSpec(memory_space=pltpu.VMEM)
    hbm = pl.BlockSpec(memory_space=pltpu.HBM)
    little = pltpu.CompilerParams(vmem_limit_bytes=8 << 20)
    params = pltpu.CompilerParams(vmem_limit_bytes=24 << 20)
    held = [
        pltpu.with_memory_space_constraint(a, pltpu.HBM)
        for a in (block_param, block_obs, omega, jac_blocks)
    ]
    rows = oblocks // ncore * probes
    each = rows // nnear
    per = each // probes
    me = lax.axis_index("core").reshape(1, 1)
    first = (lax.axis_index("core") * nnear + lax.axis_index(NEAR)) * per
    weight = lax.dynamic_slice(obs_weight.reshape(oblocks, 1, width), (first, 0, 0), (per, 1, width))
    sums, jac = pl.pallas_call(
        fwd_kernel,
        out_shape=(
            jax.ShapeDtypeStruct((ncore, rows + SUB, width), jnp.float32),
            jax.ShapeDtypeStruct((slots, width, width), jac_blocks.dtype),
        ),
        in_specs=[smem] * 2 + [hbm] * 4,
        out_specs=(vmem, vmem),
        scratch_shapes=[
            pltpu.SMEM(block_param.shape, jnp.int32),
            pltpu.SMEM(block_obs.shape, jnp.int32),
            pltpu.VMEM(omega.shape, omega.dtype),
            pltpu.SemaphoreType.DMA((3,)),
            pltpu.SemaphoreType.DMA((len(PIECES),)),
        ],
        compiler_params=params,
        name="fwd_blocks",
    )(me, block_count, *held)
    sums, weight = lax.optimization_barrier((sums, weight))

    def small_call(kernel, shape, dtype, name, in_specs):
        return pl.pallas_call(
            kernel,
            out_shape=jax.ShapeDtypeStruct(shape, dtype),
            in_specs=in_specs,
            out_specs=vmem,
            compiler_params=little,
            name=name,
        )

    got = lax.all_gather(sums[1].astype(jnp.float16), "core").astype(jnp.float32)
    packed = small_call(
        core_kernel, (nnear, each + SUB, width), jnp.float32, "add_core", [smem, vmem, vmem]
    )(me, sums, got)
    got = lax.all_to_all(packed.astype(jnp.float16), NEAR, 0, 0, tiled=True).astype(jnp.float32)
    packed = small_call(near_kernel, (each + SUB, width), jnp.float32, "add_near", [vmem])(got)
    got = lax.all_gather(packed.astype(jnp.float16), "zh").astype(jnp.float32)
    scaled = small_call(far_kernel, (nnear, each, width), jnp.bfloat16, "add_far", [vmem] * 2)(got, weight)
    scaled = lax.all_to_all(scaled, NEAR, 0, 0, tiled=True).reshape(rows, width)
    scaled = lax.all_gather(scaled, "core", axis=0, tiled=True).reshape(oblocks, probes, width)

    local_terms = pl.pallas_call(
        bwd_kernel,
        out_shape=jax.ShapeDtypeStruct((pblocks, probes, width), jnp.bfloat16),
        in_specs=[smem, smem, smem, vmem, vmem],
        out_specs=vmem,
        scratch_shapes=[pltpu.VMEM((pblocks, probes, width), jnp.float32)],
        compiler_params=params,
        name="bwd_blocks",
    )(block_count, block_param, block_obs, scaled, jac)

    n = lax.axis_size(GRP)
    got = lax.all_to_all(local_terms, GRP, 0, 0, tiled=True)
    got = got.reshape(n, pblocks // n, probes, width)
    return small_call(
        total_kernel, (probes, pblocks // n * width), jnp.float32, "add_groups", [vmem]
    )(got)


def solution(mesh):
    mesh = Mesh(mesh.devices.reshape(4, 2, 4, 4, 2, 2), GRP + PAR)
    in_specs = (
        P(None, PAR),
        P(GRP, PAR, None, None),
        P(GRP, PAR),
        P(GRP, PAR),
        P(GRP, PAR),
        P(GRP, None),
    )
    out_specs = P(None, PAR + GRP)
    return jax.shard_map(
        on_device, mesh=mesh, in_specs=in_specs, out_specs=out_specs, check_vma=False
    )
```

```python
import jax
import jax.numpy as jnp
from jax import lax
from jax.experimental import pallas as pl
from jax.experimental.pallas import tpu as pltpu
from jax.sharding import Mesh, PartitionSpec as P

CHUNK = 64
GROUP = 4
SUB = 8
PAR = ("zh", "zl", "yh", "core")
NEAR = ("zl", "yh")
GRP = ("x", "yl")


def exponent(top):
    return jnp.clip(jnp.ceil(jnp.log2(top)), -100.0, 100.0) - 14.0


def fwd_kernel(
    me, cnt, bp_hbm, bo_hbm, omega_hbm, jac_hbm, sums_ref, jac, bp, bo, omega, sems, jsems
):
    width = jac.shape[1]
    probes = omega.shape[0]
    rows = sums_ref.shape[1] - SUB
    half = rows // probes
    small = [
        pltpu.make_async_copy(src, dst, sems.at[i])
        for i, (src, dst) in enumerate(((bp_hbm, bp), (bo_hbm, bo), (omega_hbm, omega)))
    ]
    n = cnt[0, 0]

    def chunk(c):
        at = pl.ds(pl.multiple_of(c * CHUNK, CHUNK), CHUNK)
        return pltpu.make_async_copy(jac_hbm.at[0, at], jac.at[at], jsems.at[c])

    for c in range(jac.shape[0] // CHUNK):

        @pl.when(c * CHUNK < n)
        def _():
            chunk(c).start()

    for copy in small:
        copy.start()
    sums_ref[...] = jnp.zeros_like(sums_ref)
    flip = me[0, 0] * half
    for copy in small:
        copy.wait()

    def step(c, carry):
        chunk(c).wait()
        for j in range(CHUNK):
            s = c * CHUNK + j
            at = pl.multiple_of(bp[0, s] * width, width)
            panel = omega[:, pl.ds(at, width)]
            panel = jnp.where(s < n, panel, jnp.zeros_like(panel))
            term = jnp.dot(panel, jac[s], preferred_element_type=jnp.float32)
            o = bo[0, s] ^ flip
            at = pl.ds(pl.multiple_of(o % half * probes, probes), probes)
            sums_ref[o // half, at] = sums_ref[o // half, at] + term
        return carry

    lax.fori_loop(0, (n + CHUNK - 1) // CHUNK, step, 0)
    top = jnp.zeros((SUB, width), jnp.float32)
    for i in range(2):
        top = jnp.maximum(top, jnp.max(jnp.abs(sums_ref[i, :rows].reshape(rows // SUB, SUB, width)), axis=0))
    power = exponent(top)
    other = sums_ref[1, :rows].reshape(rows // SUB, SUB, width) * jnp.exp2(-power)
    sums_ref[1, :rows] = other.reshape(rows, width)
    sums_ref[0, rows:] = top
    sums_ref[1, rows:] = power


def unscaled_sum(got_ref):
    parts, each, width = got_ref.shape
    each = each - SUB
    total = None
    for i in range(parts):
        data = got_ref[i, :each].reshape(each // SUB, SUB, width) * jnp.exp2(got_ref[i, each:])
        total = data if total is None else total + data
    return total


def core_kernel(me, sums_ref, got_ref, out_ref):
    parts, each, width = out_ref.shape
    each = each - SUB
    rows = parts * each
    got = got_ref[1 - me[0, 0]]
    theirs = got[rows:]
    power = exponent(sums_ref[0, rows:] + jnp.exp2(theirs + 14.0))
    data = sums_ref[0, :rows].reshape(rows // SUB, SUB, width) * jnp.exp2(-power)
    data = data + got[:rows].reshape(rows // SUB, SUB, width) * jnp.exp2(theirs - power)
    out_ref[:, :each] = data.reshape(parts, each, width)
    out_ref[:, each:] = jnp.broadcast_to(power, (parts, SUB, width))


def near_kernel(got_ref, out_ref):
    rows, width = out_ref.shape
    rows = rows - SUB
    total = unscaled_sum(got_ref)
    power = exponent(jnp.max(jnp.abs(total), axis=0))
    out_ref[:rows] = (total * jnp.exp2(-power)).reshape(rows, width)
    out_ref[rows:] = power


def far_kernel(got_ref, weight_ref, out_ref):
    copies, rows, width = out_ref.shape
    per = weight_ref.shape[0]
    total = unscaled_sum(got_ref).reshape(per, rows // per, width)
    scaled = (total * weight_ref[...]).reshape(rows, width).astype(out_ref.dtype)
    out_ref[...] = jnp.broadcast_to(scaled, (copies, rows, width))


def total_kernel(got_ref, out_ref):
    parts, blocks, _, width = got_ref.shape
    for j in range(blocks):
        total = got_ref[0, j].astype(jnp.float32)
        for i in range(1, parts):
            total = total + got_ref[i, j].astype(jnp.float32)
        out_ref[:, j * width : (j + 1) * width] = total


def bwd_kernel(cnt, bp, bo, v_ref, jac, out_ref, acc):
    width = jac.shape[1]
    probes = v_ref.shape[1]
    n = cnt[0, 0]
    acc[...] = jnp.zeros_like(acc)

    def step(c, carry):
        for j in range(0, CHUNK, GROUP):
            first = c * CHUNK + j
            group = []
            for s in range(GROUP):
                s = first + s
                v = v_ref[bo[0, s]]
                group.append(jnp.where(s < n, v, jnp.zeros_like(v)))
            blocks = jac[pl.ds(first, GROUP)].reshape(GROUP * width, width)
            terms = lax.dot_general(
                jnp.concatenate(group, axis=0),
                blocks,
                (((1,), (1,)), ((), ())),
                preferred_element_type=jnp.float32,
            )
            for i in range(GROUP):
                p = bp[0, first + i]
                acc[p] = acc[p] + terms[i * probes : (i + 1) * probes, i * width : (i + 1) * width]
        return carry

    lax.fori_loop(0, (n + CHUNK - 1) // CHUNK, step, 0)
    out_ref[...] = acc[...].astype(out_ref.dtype)


def on_device(omega, jac_blocks, block_param, block_obs, block_count, obs_weight):
    probes = omega.shape[0]
    slots, width = jac_blocks.shape[1], jac_blocks.shape[2]
    pblocks = omega.shape[1] // width
    oblocks = obs_weight.shape[1] // width
    ncore, nnear = lax.axis_size("core"), lax.axis_size(NEAR)
    smem = pl.BlockSpec(memory_space=pltpu.SMEM)
    vmem = pl.BlockSpec(memory_space=pltpu.VMEM)
    hbm = pl.BlockSpec(memory_space=pltpu.HBM)
    little = pltpu.CompilerParams(vmem_limit_bytes=8 << 20)
    params = pltpu.CompilerParams(vmem_limit_bytes=24 << 20)
    held = [
        pltpu.with_memory_space_constraint(a, pltpu.HBM)
        for a in (block_param, block_obs, omega, jac_blocks)
    ]
    rows = oblocks // ncore * probes
    each = rows // nnear
    per = each // probes
    me = lax.axis_index("core").reshape(1, 1)
    first = (lax.axis_index("core") * nnear + lax.axis_index(NEAR)) * per
    weight = lax.dynamic_slice(obs_weight.reshape(oblocks, 1, width), (first, 0, 0), (per, 1, width))
    sums, jac = pl.pallas_call(
        fwd_kernel,
        out_shape=(
            jax.ShapeDtypeStruct((ncore, rows + SUB, width), jnp.float32),
            jax.ShapeDtypeStruct((slots, width, width), jac_blocks.dtype),
        ),
        in_specs=[smem] * 2 + [hbm] * 4,
        out_specs=(vmem, vmem),
        scratch_shapes=[
            pltpu.SMEM(block_param.shape, jnp.int32),
            pltpu.SMEM(block_obs.shape, jnp.int32),
            pltpu.VMEM(omega.shape, omega.dtype),
            pltpu.SemaphoreType.DMA((3,)),
            pltpu.SemaphoreType.DMA((slots // CHUNK,)),
        ],
        compiler_params=params,
        name="fwd_blocks",
    )(me, block_count, *held)
    sums, weight = lax.optimization_barrier((sums, weight))

    def small_call(kernel, shape, dtype, name, in_specs):
        return pl.pallas_call(
            kernel,
            out_shape=jax.ShapeDtypeStruct(shape, dtype),
            in_specs=in_specs,
            out_specs=vmem,
            compiler_params=little,
            name=name,
        )

    got = lax.all_gather(sums[1].astype(jnp.float16), "core").astype(jnp.float32)
    packed = small_call(
        core_kernel, (nnear, each + SUB, width), jnp.float32, "add_core", [smem, vmem, vmem]
    )(me, sums, got)
    got = lax.all_to_all(packed.astype(jnp.float16), NEAR, 0, 0, tiled=True).astype(jnp.float32)
    packed = small_call(near_kernel, (each + SUB, width), jnp.float32, "add_near", [vmem])(got)
    got = lax.all_gather(packed.astype(jnp.float16), "zh").astype(jnp.float32)
    scaled = small_call(far_kernel, (nnear, each, width), jnp.bfloat16, "add_far", [vmem] * 2)(got, weight)
    scaled = lax.all_to_all(scaled, NEAR, 0, 0, tiled=True).reshape(rows, width)
    scaled = lax.all_gather(scaled, "core", axis=0, tiled=True).reshape(oblocks, probes, width)

    local_terms = pl.pallas_call(
        bwd_kernel,
        out_shape=jax.ShapeDtypeStruct((pblocks, probes, width), jnp.bfloat16),
        in_specs=[smem, smem, smem, vmem, vmem],
        out_specs=vmem,
        scratch_shapes=[pltpu.VMEM((pblocks, probes, width), jnp.float32)],
        compiler_params=params,
        name="bwd_blocks",
    )(block_count, block_param, block_obs, scaled, jac)

    n = lax.axis_size(GRP)
    got = lax.all_to_all(local_terms, GRP, 0, 0, tiled=True)
    got = got.reshape(n, pblocks // n, probes, width)
    return small_call(
        total_kernel, (probes, pblocks // n * width), jnp.float32, "add_groups", [vmem]
    )(got)


def solution(mesh):
    mesh = Mesh(mesh.devices.reshape(4, 2, 4, 4, 2, 2), GRP + PAR)
    in_specs = (
        P(None, PAR),
        P(GRP, PAR, None, None),
        P(GRP, PAR),
        P(GRP, PAR),
        P(GRP, PAR),
        P(GRP, None),
    )
    out_specs = P(None, PAR + GRP)
    return jax.shard_map(
        on_device, mesh=mesh, in_specs=in_specs, out_specs=out_specs, check_vma=False
    )
```
